256 devices in a mesh: sta: 64 (over x, z, core), seg: 4 (over y).
Axes of the slice: x: 4, y: 4, z: 8, core: 2. Of those that a mesh axis runs over, the one named last changes fastest.
Arguments:
- traces: float32 [1024, 8, 4096], P('sta', 'seg'), may hold values from -60 to 60, as said below
- pair_blocks: int32 [2048, 2], P('sta'), may hold values from 0 to 255, as said below
- pair_counts: int32 [64], P('sta'), may hold values from 4 to 32, as said below
Outputs:
- correlations: bfloat16 [2048, 4, 4, 4096], P(('sta', 'seg'))
The draws below stay inside these ranges and needn't reach their ends.
Inputs may be any that keep to these rules, and one draw needn't show every extreme that they name: `traces`: random scales per station. `pair_blocks`: rows k * 32 to (k + 1) * 32 - 1 belong to owner k: their first block is one of owner k's stations' blocks, numbers k * 4 to (k + 1) * 4 - 1. Over the 32 rows of one owner, at most 1 second blocks lie in the blocks of any one index of sta, and every owner has exactly 1 for some index. `pair_counts`: one owner has exactly 32 live slots; live slots are the first ones of an owner.
All inputs are finite; a program needn't handle non-finite values.
Results may differ from the reference program's by a relative error of at most 0.0057.
Values may be sent and summed in bfloat16 or wider, within the bound.
A program may use at most 128 MiB of HBM per device.

```python
import math
import jax
import jax.numpy as jnp
from jax import lax

L = 4096
F = 2048
BLK = 4
SEGS = 8
S_DEV = 16
PAIR_DEV = 32
STATIONS = 1024
BLOCKS = 256
SLOTS = 2048
CAP = 1
N_STA = 64


def draw_traces(key, part):
    key_scale, key_noise = jax.random.split(key, 2)
    log_scale = jax.random.uniform(key_scale, (STATIONS, 1, 1), jnp.float32, 0.0, math.log(10.0))
    station_scale = jnp.exp(log_scale)
    noise_part = jnp.clip(jax.random.normal(key_noise, (STATIONS, SEGS, L), jnp.float32), -6.0, 6.0)
    return (station_scale * noise_part).astype(jnp.float32)


def draw_pair_blocks(key, part):
    block_count = S_DEV // BLK

    def one_owner(owner):
        owner_key = jax.random.fold_in(key, owner)
        key_perm, key_order, key_first, key_second = jax.random.split(owner_key, 4)
        shuffled = jax.random.permutation(key_perm, CAP * N_STA)
        homes = shuffled // CAP
        leading_home = homes[0]
        scores = jnp.where(homes == leading_home, -1, jnp.arange(CAP * N_STA))
        ordering = jnp.argsort(scores, stable=True)
        chosen = homes[ordering][:PAIR_DEV]
        chosen = jax.random.permutation(key_order, chosen)
        local_first = jax.random.randint(key_first, (PAIR_DEV,), 0, block_count)
        local_second = jax.random.randint(key_second, (PAIR_DEV,), 0, block_count)
        return jnp.stack([owner * block_count + local_first, chosen * block_count + local_second], axis=1)
    result = jax.vmap(one_owner)(jnp.arange(N_STA))
    return result.reshape(N_STA * PAIR_DEV, 2).astype(jnp.int32)


def draw_pair_counts(key, part):
    key_counts, key_full = jax.random.split(jax.random.fold_in(key, 7), 2)
    counts = jax.random.randint(key_counts, (N_STA,), PAIR_DEV // 8, 3 * PAIR_DEV // 4 + 1)
    full_owner = jax.random.randint(key_full, (), 0, N_STA)
    return jnp.where(jnp.arange(N_STA) == full_owner, PAIR_DEV, counts).astype(jnp.int32)


def setup_inputs(seed: int = 0) -> dict:
    streams_of = jax.random.split(jax.random.key(seed), 4)
    traces = draw_traces(jax.random.fold_in(streams_of[3], 71), 0)
    pair_blocks = draw_pair_blocks(jax.random.fold_in(streams_of[3], 71), 0)
    pair_counts = draw_pair_counts(jax.random.fold_in(streams_of[3], 71), 0)
    return dict(traces=traces, pair_blocks=pair_blocks, pair_counts=pair_counts)


band_count = 32
epsilon = 1e-06

def whitened(traces):
    centred = traces - lax.optimization_barrier(jnp.mean(traces, axis=-1, keepdims=True))
    spectrum = jnp.fft.rfft(centred, axis=-1)[..., :L // 2]
    real_part = jnp.real(spectrum)
    imag_part = jnp.imag(spectrum)
    leading = traces.shape[:-1]
    band_power = (real_part * real_part + imag_part * imag_part).reshape(leading + (band_count, -1))
    inverse_amp = 1.0 / jnp.sqrt(lax.optimization_barrier(jnp.mean(band_power, axis=-1, keepdims=True)) + epsilon)
    white_real = (real_part.reshape(leading + (band_count, -1)) * inverse_amp).reshape(leading + (-1,))
    white_imag = (imag_part.reshape(leading + (band_count, -1)) * inverse_amp).reshape(leading + (-1,))
    return (white_real.astype(jnp.bfloat16), white_imag.astype(jnp.bfloat16))

def reference(traces, pair_blocks, pair_counts):
    white_real, white_imag = whitened(traces)
    block_real = white_real.reshape(BLOCKS, BLK, SEGS, F)
    block_imag = white_imag.reshape(BLOCKS, BLK, SEGS, F)
    owner_pairs = pair_blocks.reshape(N_STA, PAIR_DEV, 2)
    highest = lax.Precision.HIGHEST

    def contract(one_side, other_side):
        return jnp.einsum('pisf,pjsf->pijf', one_side, other_side, precision=highest)

    def per_owner(packed):
        slot_pairs, live_count = packed
        first_real = block_real[slot_pairs[:, 0]].astype(jnp.float32)
        first_imag = block_imag[slot_pairs[:, 0]].astype(jnp.float32)
        second_real = block_real[slot_pairs[:, 1]].astype(jnp.float32)
        second_imag = block_imag[slot_pairs[:, 1]].astype(jnp.float32)
        cross_real = contract(first_real, second_real) + contract(first_imag, second_imag)
        cross_imag = contract(first_imag, second_real) - contract(first_real, second_imag)
        live_mask = (jnp.arange(PAIR_DEV) < live_count).astype(jnp.float32)[:, None, None, None]
        cross_spec = (cross_real + 1j * cross_imag) * live_mask
        padded = jnp.concatenate([cross_spec, jnp.zeros(cross_spec.shape[:-1] + (1,), cross_spec.dtype)], axis=-1)
        series = jnp.fft.irfft(padded, n=L, axis=-1) * (L / math.sqrt(F * SEGS))
        return series.astype(jnp.bfloat16)
    stacked = lax.map(per_owner, (owner_pairs, pair_counts))
    return stacked.reshape(SLOTS, BLK, BLK, L)
```

```python
import functools
import math

import jax
import jax.numpy as jnp
import ml_dtypes
import numpy as np
from jax import lax
from jax.experimental import pallas as pl
from jax.experimental.pallas import tpu as pltpu
from jax.sharding import PartitionSpec as P

MESH = pl.DeviceIdType.MESH
F32 = jnp.float32
BF16 = jnp.bfloat16
HIGHEST = lax.Precision.HIGHEST
EPSILON = 1e-06
NX, NZ, NY = 4, 8, 4
CHUNKS = 4
SLOTS = 32
MIB = 1 << 20


def split_high(table):
    high = table.astype(ml_dtypes.bfloat16)
    return high, (table - high.astype(np.float64)).astype(ml_dtypes.bfloat16)


def forward_tables():
    a = np.arange(32)
    outer = np.zeros((2, 16, 2, 4, 2, 4, 32, 2))
    for c in range(16):
        for e in range(2):
            angle = 2 * np.pi * (a * (2 * c + e) % 32) / 32
            for g in range(2):
                for j in range(4):
                    outer[0, c, g, j, e, j, :, g] = np.cos(angle)
                    outer[1, c, g, j, e, j, :, g] = -np.sin(angle)
    k = np.broadcast_to(2 * np.arange(16)[:, None, None] + np.arange(2), (16, 8, 2)).reshape(256)
    twist = 2 * np.pi * (k[:, None] * np.arange(128)) / 4096
    inner = 2 * np.pi * (np.arange(128)[:, None] * np.arange(64) % 128) / 128
    cos, sin = np.cos(inner), np.sin(inner)
    inner = np.concatenate([np.concatenate([cos, -sin], 1), np.concatenate([sin, cos], 1)], 0)
    return tuple(
        t.astype(np.float32) for t in (outer.reshape(512, 256), np.cos(twist), np.sin(twist), inner)
    )


def inverse_tables():
    inner = 2 * np.pi * (np.arange(64)[:, None] * np.arange(128) % 128) / 128
    cos, sin = np.cos(inner) / 64, np.sin(inner) / 64
    inner = np.concatenate([np.concatenate([cos, sin], 1), np.concatenate([-sin, cos], 1)], 0)
    inner = np.concatenate(split_high(inner), 0)
    k = np.broadcast_to(2 * np.arange(16)[:, None, None] + np.arange(2), (16, 4, 2)).reshape(16, 8)
    twist = 2 * np.pi * (k[:, :, None] * np.arange(128)) / 4096
    outer = np.zeros((32, 4, 2, 16, 4, 2))
    u = np.arange(32)
    for c in range(16):
        for e in range(2):
            angle = 2 * np.pi * (u * (2 * c + e) % 32) / 32
            for j in range(4):
                outer[:, j, 0, c, j, e] = np.cos(angle)
                outer[:, j, 1, c, j, e] = -np.sin(angle)
    high, low = split_high(outer.reshape(128, 256))
    outer = np.concatenate([high, high, low], 1)
    weight = np.ones((32, 128))
    weight[::2, 0] = 0.5
    return (
        inner,
        np.cos(twist).astype(np.float32),
        np.sin(twist).astype(np.float32),
        outer,
        weight.astype(ml_dtypes.bfloat16),
    )


def whiten_kernel(x_ref, pairs_ref, outer_ref, cos_ref, sin_ref, inner_ref, white_ref, need_ref):
    x = x_ref[...].reshape(16, 8, 8, 128)
    total = jnp.sum(x, axis=1)
    total = total + pltpu.roll(total, 4, 1)
    total = total + pltpu.roll(total, 2, 1)
    mean = jnp.sum(total, axis=-1, keepdims=True) * (1.0 / 4096)
    x = (x - mean[:, None]).reshape(4, 256, 128)
    row = lax.broadcasted_iota(jnp.int32, (2, 8, 128), 1)
    lane = lax.broadcasted_iota(jnp.int32, (2, 8, 128), 2)
    cos, sin = cos_ref[...], sin_ref[...]
    for half in range(2):
        both = jnp.concatenate([x[2 * half], x[2 * half + 1]], axis=1)
        section = jnp.dot(outer_ref[...], both, precision=HIGHEST, preferred_element_type=F32)
        for b in range(2):
            real = section[:256, 128 * b : 128 * b + 128]
            imag = section[256:, 128 * b : 128 * b + 128]
            turned = jnp.concatenate([real * cos + imag * sin, imag * cos - real * sin], axis=1)
            spec = jnp.dot(turned, inner_ref[...], precision=HIGHEST, preferred_element_type=F32)
            spec = spec.reshape(16, 2, 8, 128)
            power = jnp.sum(spec * spec, axis=0)
            power = power + jnp.where(row % 2 == 0, pltpu.roll(power, 7, 1), pltpu.roll(power, 1, 1))
            power = power + jnp.where(lane % 2 == 0, pltpu.roll(power, 127, 2), pltpu.roll(power, 1, 2))
            power = power + pltpu.roll(power, 64, 2)
            white = spec * (1.0 / jnp.sqrt(power * (1.0 / 64) + EPSILON))
            white_ref[:, :, 2 * half + b] = white.reshape(4, 4, 16, 128).astype(BF16)
    partner = pairs_ref[:, 1:2]
    source = lax.broadcasted_iota(jnp.int32, (SLOTS, 128), 1)
    need = jnp.sum(jnp.where(partner // 4 == source, partner % 4, 0), axis=0, keepdims=True)
    need_ref[...] = jnp.broadcast_to(need, (8, 128))


def exchange_kernel(
    white_ref,
    need_ref,
    pairs_ref,
    stacked_ref,
    *scratch,
):
    ring, chosen = scratch[:CHUNKS], scratch[CHUNKS : 2 * CHUNKS]
    picked, sides, cross, table, lookup, need_sem, table_sem, own_sem, y_sem, z_sem, x_sem, c_sem, keep_sem = scratch[
        2 * CHUNKS :
    ]
    sta, q = lax.axis_index("sta"), lax.axis_index("seg")
    x, z, core = sta // 16, sta // 2 % 8, sta % 2

    def at(dx, dz, flip):
        other = core if flip == 0 else 1 - core
        return (((x + dx) % NX * NZ + (z + dz) % NZ) * 2 + other, q)

    def along(dy):
        return (sta, (q + dy) % NY)

    row_peers = [(d, f) for d in range(NX) for f in range(2) if (d, f) != (0, 0)]
    targets = [along(r) for r in range(1, NY)] + [at(0, 1, 0), at(0, NZ - 1, 0)]
    targets += [at(d, 0, f) for d, f in row_peers]
    barrier = pltpu.get_barrier_semaphore()
    for target in targets:
        pl.semaphore_signal(barrier, inc=1, device_id=target, device_id_type=MESH)
    pl.semaphore_wait(barrier, len(targets))

    started = []

    def send(source, destination, sems, target):
        copy = pltpu.make_async_remote_copy(
            source, destination, sems.at[0], sems.at[1], device_id=target, device_id_type=MESH
        )
        copy.start()
        started.append(copy)
        return copy

    own = []
    y_in = [[] for _ in range(CHUNKS)]
    for c in range(CHUNKS):
        for r in range(1, NY):
            y_in[c].append(
                send(white_ref.at[(q + r) % NY, c], ring[c].at[0, r], y_sem.at[c, r], along(r))
            )
        copy = pltpu.make_async_copy(white_ref.at[q, c], ring[c].at[0, 0], own_sem.at[c])
        copy.start()
        own.append(copy)
    need_in = [
        send(need_ref, table.at[d * 2 + f], need_sem.at[d * 2 + f], at(d, 0, f)) for d, f in row_peers
    ]
    table[0] = need_ref[...]

    def gather_ring(c):
        own[c].wait()
        for copy in y_in[c]:
            copy.wait_recv()
        for t in range(1, 5):
            copies = []
            if t < 4 or c % 2 == 0:
                copies.append(send(ring[c].at[t - 1], ring[c].at[t], z_sem.at[c, t], at(0, 1, 0)))
            if t < 4 or c % 2 == 1:
                copies.append(
                    send(ring[c].at[(9 - t) % 8], ring[c].at[8 - t], z_sem.at[c, 8 - t], at(0, NZ - 1, 0))
                )
            for copy in copies:
                copy.wait_recv()

    def pick(c):
        def one(slot, carry):
            for dz in range(NZ):
                block = lookup[slot, 0, (x * NZ + (z - dz) % NZ) * 2 + core]
                picked[c, slot, dz] = ring[c][dz, :, block]
            return carry

        lax.fori_loop(0, 2 * NX, one, 0)
        chosen[c][0] = picked[c, 0]

    def spread(c):
        return [
            send(picked.at[c, d * 2 + f], chosen[c].at[(NX - d) % NX * 2 + f], x_sem.at[c, d * 2 + f], at(-d, 0, f))
            for d, f in row_peers
        ]

    row = lax.broadcasted_iota(jnp.int32, (8, 128), 0)
    left = lax.broadcasted_iota(jnp.int32, (8, 128), 1) < 64

    def prepare(c):
        def one(step, carry):
            b, r = step // NY, step % NY
            both = ring[c][0, r, b].astype(F32)
            for g in range(2):
                value = both[8 * g : 8 * g + 8]
                turned = pltpu.roll(value, 64, 1)
                for part, side in enumerate(
                    (jnp.where(left, value, -turned), jnp.where(left, turned, value))
                ):
                    for i in range(4):
                        only = jnp.where(row // 2 == i, side, 0.0)
                        only = only + pltpu.roll(only, 2, 0)
                        sides[b, part, i, r * 2 + g] = only + pltpu.roll(only, 4, 0)
            return carry

        lax.fori_loop(0, 4 * NY, one, 0)

    def multiply(c):
        def one(slot, carry):
            first = pairs_ref[slot, 0] % 4
            partner = pairs_ref[slot, 1] // 4
            dx, dz, flip = (x - partner // 16) % NX, (z - partner // 2 % 8) % NZ, (core + partner) % 2
            second = chosen[c][dx * 2 + flip, dz].astype(F32)
            rows = []
            for i in range(4):
                straight = sides[first, 0, i, 0] * second[0, 0:8]
                crossed = sides[first, 1, i, 0] * second[0, 0:8]
                for g in range(1, 8):
                    part = second[g // 2, 8 * (g % 2) : 8 * (g % 2) + 8]
                    straight = straight + sides[first, 0, i, g] * part
                    crossed = crossed + sides[first, 1, i, g] * part
                rows.append(straight + pltpu.roll(crossed, 64, 1))
            cross[c, slot] = jnp.concatenate(rows, axis=0).astype(BF16)
            return carry

        lax.fori_loop(0, SLOTS, one, 0)

    last = []

    def hand_over(c):
        for r in range(1, NY):
            last.append(
                send(
                    cross.at[c, pl.ds((q + r) % NY * 8, 8)],
                    stacked_ref.at[q, c],
                    c_sem.at[c, r],
                    along(r),
                )
            )
        copy = pltpu.make_async_copy(cross.at[c, pl.ds(q * 8, 8)], stacked_ref.at[q, c], keep_sem.at[c])
        copy.start()
        return copy

    kept = []
    x_in = {}

    def finish(c):
        prepare(c)
        for copy in x_in[c]:
            copy.wait_recv()
        multiply(c)
        kept.append(hand_over(c))

    gather_ring(0)
    for copy in need_in:
        copy.wait_recv()
    copy = pltpu.make_async_copy(table, lookup, table_sem)
    copy.start()
    copy.wait()
    for c in range(CHUNKS):
        if c:
            gather_ring(c)
        pick(c)
        x_in[c] = spread(c)
        if c:
            finish(c - 1)
    finish(CHUNKS - 1)
    for copy in kept:
        copy.wait()
    for copy in last:
        copy.wait_recv()
    for copy in started:
        copy.wait_send()


def invert_kernel(counts_ref, stacked_ref, inner_ref, cos_ref, sin_ref, outer_ref, weight_ref, out_ref):
    slot = lax.axis_index("seg") * 8 + pl.program_id(0)
    live = (slot < counts_ref[0]).astype(F32)
    cross = stacked_ref[:, :, 0].reshape(16, 32, 128)
    cross = jnp.concatenate([cross[0:1] * weight_ref[...], cross[1:]], axis=0).reshape(512, 128)
    series = jnp.dot(jnp.concatenate([cross, cross], axis=1), inner_ref[...], preferred_element_type=F32)
    series = series.reshape(16, 4, 8, 256)
    cos, sin = cos_ref[...] * live, sin_ref[...] * live
    parts = []
    for i in range(4):
        real, imag = series[:, i, :, :128], series[:, i, :, 128:]
        turned = jnp.concatenate(
            [(real * cos - imag * sin).reshape(128, 128), (real * sin + imag * cos).reshape(128, 128)], axis=0
        )
        parts.append(turned)
    for pair in range(2):
        both = jnp.concatenate([parts[2 * pair], parts[2 * pair + 1]], axis=1)
        high = both.astype(BF16)
        low = (both - high.astype(F32)).astype(BF16)
        lags = jnp.dot(
            outer_ref[...], jnp.concatenate([high, low, high], axis=0), preferred_element_type=F32
        ).astype(BF16)
        out_ref[0, 2 * pair] = lags[:, :128]
        out_ref[0, 2 * pair + 1] = lags[:, 128:]


def vmem():
    return pl.BlockSpec(memory_space=pltpu.VMEM)


def local(traces, pair_blocks, pair_counts):
    stations, segs, length = traces.shape
    rows = traces.reshape(stations, segs, 32, 128).transpose(0, 2, 1, 3).reshape(1024, 128)
    white, need = pl.pallas_call(
        whiten_kernel,
        out_shape=(
            jax.ShapeDtypeStruct((NY, CHUNKS, 4, 16, 128), BF16),
            jax.ShapeDtypeStruct((8, 128), jnp.int32),
        ),
        in_specs=[vmem()] * 6,
        out_specs=(vmem(), vmem()),
        compiler_params=pltpu.CompilerParams(vmem_limit_bytes=32 * MIB),
        name="whiten",
    )(rows, pair_blocks, *forward_tables())
    dma = pltpu.SemaphoreType.DMA
    stacked = pl.pallas_call(
        exchange_kernel,
        out_shape=jax.ShapeDtypeStruct((NY, CHUNKS, 8, 32, 128), BF16),
        in_specs=[vmem(), vmem(), pl.BlockSpec(memory_space=pltpu.SMEM)],
        out_specs=pl.BlockSpec(memory_space=pl.ANY),
        scratch_shapes=[
            *[pltpu.VMEM((NZ, NY, 4, 16, 128), BF16)] * CHUNKS,
            *[pltpu.VMEM((2 * NX, NZ, NY, 16, 128), BF16)] * CHUNKS,
            pltpu.VMEM((CHUNKS, 2 * NX, NZ, NY, 16, 128), BF16),
            pltpu.VMEM((4, 2, 4, 8, 8, 128), F32),
            pltpu.VMEM((CHUNKS, SLOTS, 32, 128), BF16),
            pltpu.VMEM((2 * NX, 8, 128), jnp.int32),
            pltpu.SMEM((2 * NX, 8, 128), jnp.int32),
            dma((2 * NX, 2)),
            dma(()),
            dma((CHUNKS,)),
            dma((CHUNKS, NY, 2)),
            dma((CHUNKS, NZ, 2)),
            dma((CHUNKS, 2 * NX, 2)),
            dma((CHUNKS, NY, 2)),
            dma((CHUNKS,)),
        ],
        compiler_params=pltpu.CompilerParams(
            collective_id=0, has_side_effects=True, vmem_limit_bytes=40 * MIB
        ),
        name="exchange",
    )(white, need, pair_blocks)
    whole = lambda *shape: pl.BlockSpec(shape, lambda p: (0,) * len(shape))
    lags = pl.pallas_call(
        invert_kernel,
        out_shape=jax.ShapeDtypeStruct((8, 4, 128, 128), BF16),
        grid=(8,),
        in_specs=[
            pl.BlockSpec(memory_space=pltpu.SMEM),
            pl.BlockSpec((NY, CHUNKS, 1, 32, 128), lambda p: (0, 0, p, 0, 0)),
            whole(256, 256),
            whole(16, 8, 128),
            whole(16, 8, 128),
            whole(128, 768),
            whole(32, 128),
        ],
        out_specs=pl.BlockSpec((1, 4, 128, 128), lambda p: (p, 0, 0, 0)),
        compiler_params=pltpu.CompilerParams(vmem_limit_bytes=32 * MIB),
        name="invert",
    )(pair_counts, stacked, *inverse_tables())
    return lags.reshape(8, 4, 32, 4, 128).transpose(0, 1, 3, 2, 4).reshape(8, 4, 4, length)


def solution(mesh):
    in_specs = (P("sta", "seg", None), P("sta", None), P("sta"))
    out_specs = P(("sta", "seg"), None, None, None)
    return jax.shard_map(local, mesh=mesh, in_specs=in_specs, out_specs=out_specs, check_vma=False)
```

```python
import functools
import math

import jax
import jax.numpy as jnp
import ml_dtypes
import numpy as np
from jax import lax
from jax.experimental import pallas as pl
from jax.experimental.pallas import tpu as pltpu
from jax.sharding import PartitionSpec as P

MESH = pl.DeviceIdType.MESH
F32 = jnp.float32
BF16 = jnp.bfloat16
HIGHEST = lax.Precision.HIGHEST
EPSILON = 1e-06
NX, NZ, NY = 4, 8, 4
CHUNKS = 4
RINGS = 3
ORDER = (0, 3, 1, 2)
SLOTS = 32
MIB = 1 << 20


def split_high(table):
    high = table.astype(ml_dtypes.bfloat16)
    return high, (table - high.astype(np.float64)).astype(ml_dtypes.bfloat16)


def forward_tables():
    a = np.arange(32)
    outer = np.zeros((2, 16, 2, 4, 2, 4, 32, 2))
    for c in range(16):
        for e in range(2):
            angle = 2 * np.pi * (a * (2 * c + e) % 32) / 32
            for g in range(2):
                for j in range(4):
                    outer[0, c, g, j, e, j, :, g] = np.cos(angle)
                    outer[1, c, g, j, e, j, :, g] = -np.sin(angle)
    k = np.broadcast_to(2 * np.arange(16)[:, None, None] + np.arange(2), (16, 8, 2)).reshape(256)
    twist = 2 * np.pi * (k[:, None] * np.arange(128)) / 4096
    inner = 2 * np.pi * (np.arange(128)[:, None] * np.arange(64) % 128) / 128
    cos, sin = np.cos(inner), np.sin(inner)
    inner = np.concatenate([np.concatenate([cos, -sin], 1), np.concatenate([sin, cos], 1)], 0)
    return tuple(
        t.astype(np.float32) for t in (outer.reshape(512, 256), np.cos(twist), np.sin(twist), inner)
    )


def inverse_tables():
    inner = 2 * np.pi * (np.arange(64)[:, None] * np.arange(128) % 128) / 128
    cos, sin = np.cos(inner) / 64, np.sin(inner) / 64
    inner = np.concatenate([np.concatenate([cos, sin], 1), np.concatenate([-sin, cos], 1)], 0)
    inner = np.concatenate(split_high(inner), 0)
    k = np.broadcast_to(2 * np.arange(16)[:, None, None] + np.arange(2), (16, 4, 2)).reshape(16, 8)
    twist = 2 * np.pi * (k[:, :, None] * np.arange(128)) / 4096
    outer = np.zeros((32, 4, 2, 16, 4, 2))
    u = np.arange(32)
    for c in range(16):
        for e in range(2):
            angle = 2 * np.pi * (u * (2 * c + e) % 32) / 32
            for j in range(4):
                outer[:, j, 0, c, j, e] = np.cos(angle)
                outer[:, j, 1, c, j, e] = -np.sin(angle)
    high, low = split_high(outer.reshape(128, 256))
    outer = np.concatenate([high, high, low], 1)
    weight = np.ones((32, 128))
    weight[::2, 0] = 0.5
    return (
        inner,
        np.cos(twist).astype(np.float32),
        np.sin(twist).astype(np.float32),
        outer,
        weight.astype(ml_dtypes.bfloat16),
    )


def whiten_kernel(x_ref, pairs_ref, outer_ref, cos_ref, sin_ref, inner_ref, white_ref, need_ref):
    x = x_ref[...].reshape(16, 8, 8, 128)
    total = jnp.sum(x, axis=1)
    total = total + pltpu.roll(total, 4, 1)
    total = total + pltpu.roll(total, 2, 1)
    mean = jnp.sum(total, axis=-1, keepdims=True) * (1.0 / 4096)
    x = (x - mean[:, None]).reshape(4, 256, 128)
    row = lax.broadcasted_iota(jnp.int32, (2, 8, 128), 1)
    lane = lax.broadcasted_iota(jnp.int32, (2, 8, 128), 2)
    cos, sin = cos_ref[...], sin_ref[...]
    for half in range(2):
        both = jnp.concatenate([x[2 * half], x[2 * half + 1]], axis=1)
        section = jnp.dot(outer_ref[...], both, precision=HIGHEST, preferred_element_type=F32)
        for b in range(2):
            real = section[:256, 128 * b : 128 * b + 128]
            imag = section[256:, 128 * b : 128 * b + 128]
            turned = jnp.concatenate([real * cos + imag * sin, imag * cos - real * sin], axis=1)
            spec = jnp.dot(turned, inner_ref[...], precision=HIGHEST, preferred_element_type=F32)
            spec = spec.reshape(16, 2, 8, 128)
            power = jnp.sum(spec * spec, axis=0)
            power = power + jnp.where(row % 2 == 0, pltpu.roll(power, 7, 1), pltpu.roll(power, 1, 1))
            power = power + jnp.where(lane % 2 == 0, pltpu.roll(power, 127, 2), pltpu.roll(power, 1, 2))
            power = power + pltpu.roll(power, 64, 2)
            white = spec * (1.0 / jnp.sqrt(power * (1.0 / 64) + EPSILON))
            white_ref[:, :, 2 * half + b] = white.reshape(4, 4, 16, 128).astype(BF16)
    partner = pairs_ref[:, 1:2]
    source = lax.broadcasted_iota(jnp.int32, (SLOTS, 128), 1)
    need = jnp.sum(jnp.where(partner // 4 == source, partner % 4, 0), axis=0, keepdims=True)
    need_ref[...] = jnp.broadcast_to(need, (8, 128))


def exchange_kernel(white_ref, need_ref, pairs_ref, stacked_ref, *scratch):
    ring, chosen = scratch[:RINGS], scratch[RINGS : RINGS + CHUNKS]
    group, picked, bounce, sides, cross, table, lookup = scratch[RINGS + CHUNKS : RINGS + CHUNKS + 7]
    need_sem, table_sem, own_sem, y_sem, z_sem, x_sem, g_sem, c_sem, keep_sem = scratch[RINGS + CHUNKS + 7 :]
    sta, q = lax.axis_index("sta"), lax.axis_index("seg")
    x, z, core = sta // 16, sta // 2 % 8, sta % 2

    def at(dx, dz, flip):
        other = core if flip == 0 else 1 - core
        return (((x + dx) % NX * NZ + (z + dz) % NZ) * 2 + other, q)

    def along(dy):
        return (sta, (q + dy) % NY)

    row_peers = [(d, f) for d in range(NX) for f in range(2) if (d, f) != (0, 0)]
    up, down, right, left = at(0, 1, 0), at(0, NZ - 1, 0), at(1, 0, 0), at(NX - 1, 0, 0)
    targets = [along(r) for r in range(1, NY)] + [up, down] + [at(d, 0, f) for d, f in row_peers]
    barrier = pltpu.get_barrier_semaphore()
    for target in targets:
        pl.semaphore_signal(barrier, inc=1, device_id=target, device_id_type=MESH)
    pl.semaphore_wait(barrier, len(targets))

    started = []

    def send(source, destination, sems, target):
        copy = pltpu.make_async_remote_copy(
            source, destination, sems.at[0], sems.at[1], device_id=target, device_id_type=MESH
        )
        copy.start()
        started.append(copy)
        return copy

    def home(c):
        return ring[c].at[0] if c < RINGS else group.at[0, 0]

    own, y_in = {}, {}
    for c in ORDER:
        y_in[c] = [
            send(white_ref.at[(q + r) % NY, c], home(c).at[r], y_sem.at[c, r], along(r)) for r in range(1, NY)
        ]
        own[c] = pltpu.make_async_copy(white_ref.at[q, c], home(c).at[0], own_sem.at[c])
        own[c].start()
    need_in = [
        send(need_ref, table.at[d * 2 + f], need_sem.at[d * 2 + f], at(d, 0, f)) for d, f in row_peers
    ]
    table[0] = need_ref[...]

    def home_ready(c):
        own[c].wait()
        for copy in y_in[c]:
            copy.wait_recv()

    def landed(copies):
        for copy in copies:
            copy.wait_recv()

    hops = {}

    def hop(c, t):
        if t == 1:
            home_ready(c)
        else:
            landed(hops[c, t - 1])
        hops[c, t] = []
        if t < 4 or c % 2 == 0:
            hops[c, t].append(send(ring[c].at[t - 1], ring[c].at[t], z_sem.at[c, t], up))
        if t < 4 or c % 2 == 1:
            hops[c, t].append(send(ring[c].at[(9 - t) % 8], ring[c].at[8 - t], z_sem.at[c, 8 - t], down))

    def pick(c):
        def one(slot, carry):
            for dz in range(NZ):
                block = lookup[slot, 0, (x * NZ + (z - dz) % NZ) * 2 + core]
                picked[c, slot, dz] = ring[c][dz, :, block]
            return carry

        landed(hops[c, 4])
        lax.fori_loop(0, 2 * NX, one, 0)
        chosen[c][0] = picked[c, 0]

    arrivals, relays = {}, {}

    def spread(c):
        relays[c] = [
            send(picked.at[c, 4], bounce.at[c, 0], x_sem.at[c, 0], right),
            send(picked.at[c, 5], bounce.at[c, 1], x_sem.at[c, 1], left),
        ]
        arrivals[c] = [
            send(picked.at[c, 6], chosen[c].at[2], x_sem.at[c, 2], right),
            send(picked.at[c, 2], chosen[c].at[6], x_sem.at[c, 3], left),
            send(picked.at[c, 7], chosen[c].at[3], x_sem.at[c, 4], at(1, 0, 1)),
            send(picked.at[c, 3], chosen[c].at[7], x_sem.at[c, 5], at(NX - 1, 0, 1)),
            send(picked.at[c, 1], chosen[c].at[1], x_sem.at[c, 6], at(0, 0, 1)),
        ]

    def forward(c):
        relays[c][0].wait_recv()
        arrivals[c].append(send(bounce.at[c, 0], chosen[c].at[4], x_sem.at[c, 7], right))
        relays[c][1].wait_recv()
        arrivals[c].append(send(bounce.at[c, 1], chosen[c].at[5], x_sem.at[c, 8], at(NX - 1, 0, 1)))

    last = CHUNKS - 1
    steps = {}

    def group_start():
        home_ready(last)
        steps["x"] = [
            send(group.at[0, 0], group.at[0, 1], g_sem.at[0], right),
            send(group.at[0, 0], group.at[0, 3], g_sem.at[1], left),
        ]

    def group_across():
        steps["x"][0].wait_recv()
        one = send(group.at[0, 1, 0:2], group.at[0, 2, 0:2], g_sem.at[2], right)
        steps["x"][1].wait_recv()
        steps[0] = [one, send(group.at[0, 3, 2:4], group.at[0, 2, 2:4], g_sem.at[3], left)]

    def group_hop(t):
        landed(steps[t - 1])
        if t < 4:
            parts = (slice(0, 4), slice(0, 4))
        else:
            parts = (slice(0, 2), slice(2, 4))
        steps[t] = [
            send(group.at[t - 1, parts[0]], group.at[t, parts[0]], g_sem.at[2 * t + 2], up),
            send(group.at[(9 - t) % 8, parts[1]], group.at[8 - t, parts[1]], g_sem.at[2 * t + 3], down),
        ]

    def group_pick():
        def one(dx, carry):
            for dz in range(NZ):
                source = ((x - dx) % NX * NZ + (z - dz) % NZ) * 2 + core
                picked[last, dx, dz] = group[dz, dx, :, lookup[1, 0, source]]
                chosen[last][dx * 2, dz] = group[dz, dx, :, lookup[0, 0, source]]
            return carry

        landed(steps[4])
        lax.fori_loop(0, NX, one, 0)
        arrivals[last] = [
            send(picked.at[last, d], chosen[last].at[2 * d + 1], g_sem.at[12 + d], at(0, 0, 1)) for d in range(NX)
        ]

    row = lax.broadcasted_iota(jnp.int32, (8, 128), 0)
    first_half = lax.broadcasted_iota(jnp.int32, (8, 128), 1) < 64

    def prepare(c):
        def one(step, carry):
            b, r = step // NY, step % NY
            both = home(c)[r, b].astype(F32)
            for g in range(2):
                value = both[8 * g : 8 * g + 8]
                turned = pltpu.roll(value, 64, 1)
                for part, side in enumerate(
                    (jnp.where(first_half, value, -turned), jnp.where(first_half, turned, value))
                ):
                    for i in range(4):
                        only = jnp.where(row // 2 == i, side, 0.0)
                        only = only + pltpu.roll(only, 2, 0)
                        sides[b, part, i, r * 2 + g] = only + pltpu.roll(only, 4, 0)
            return carry

        lax.fori_loop(0, 4 * NY, one, 0)

    kept, handed = [], []

    def multiply(c):
        def one(slot, carry):
            first = pairs_ref[slot, 0] % 4
            partner = pairs_ref[slot, 1] // 4
            dx, dz, flip = (x - partner // 16) % NX, (z - partner // 2 % 8) % NZ, (core + partner) % 2
            second = chosen[c][dx * 2 + flip, dz].astype(F32)
            rows = []
            for i in range(4):
                straight = sides[first, 0, i, 0] * second[0, 0:8]
                crossed = sides[first, 1, i, 0] * second[0, 0:8]
                for g in range(1, 8):
                    part = second[g // 2, 8 * (g % 2) : 8 * (g % 2) + 8]
                    straight = straight + sides[first, 0, i, g] * part
                    crossed = crossed + sides[first, 1, i, g] * part
                rows.append(straight + pltpu.roll(crossed, 64, 1))
            cross[c, slot] = jnp.concatenate(rows, axis=0).astype(BF16)
            return carry

        landed(arrivals[c])
        lax.fori_loop(0, SLOTS, one, 0)
        for r in range(1, NY):
            part = cross.at[c, pl.ds((q + r) % NY * 8, 8)]
            handed.append(send(part, stacked_ref.at[q, c], c_sem.at[c, r], along(r)))
        copy = pltpu.make_async_copy(cross.at[c, pl.ds(q * 8, 8)], stacked_ref.at[q, c], keep_sem.at[c])
        copy.start()
        kept.append(copy)

    hop(0, 1)
    group_start()
    hop(1, 1)
    hop(0, 2)
    landed(need_in)
    copy = pltpu.make_async_copy(table, lookup, table_sem)
    copy.start()
    copy.wait()
    group_across()
    hop(2, 1)
    hop(1, 2)
    hop(0, 3)
    hop(2, 2)
    hop(1, 3)
    hop(0, 4)
    group_hop(1)
    pick(0)
    spread(0)
    hop(2, 3)
    hop(1, 4)
    pick(1)
    forward(0)
    spread(1)
    hop(2, 4)
    group_hop(2)
    prepare(0)
    pick(2)
    group_hop(3)
    multiply(0)
    prepare(1)
    forward(1)
    spread(2)
    group_hop(4)
    multiply(1)
    prepare(last)
    forward(2)
    group_pick()
    multiply(last)
    prepare(2)
    multiply(2)
    for copy in kept:
        copy.wait()
    landed(handed)
    for copy in started:
        copy.wait_send()


def invert_kernel(counts_ref, stacked_ref, inner_ref, cos_ref, sin_ref, outer_ref, weight_ref, out_ref):
    slot = lax.axis_index("seg") * 8 + pl.program_id(0)
    live = (slot < counts_ref[0]).astype(F32)
    cross = stacked_ref[:, :, 0].reshape(16, 32, 128)
    cross = jnp.concatenate([cross[0:1] * weight_ref[...], cross[1:]], axis=0).reshape(512, 128)
    series = jnp.dot(jnp.concatenate([cross, cross], axis=1), inner_ref[...], preferred_element_type=F32)
    series = series.reshape(16, 4, 8, 256)
    cos, sin = cos_ref[...] * live, sin_ref[...] * live
    parts = []
    for i in range(4):
        real, imag = series[:, i, :, :128], series[:, i, :, 128:]
        turned = jnp.concatenate(
            [(real * cos - imag * sin).reshape(128, 128), (real * sin + imag * cos).reshape(128, 128)], axis=0
        )
        parts.append(turned)
    for pair in range(2):
        both = jnp.concatenate([parts[2 * pair], parts[2 * pair + 1]], axis=1)
        high = both.astype(BF16)
        low = (both - high.astype(F32)).astype(BF16)
        lags = jnp.dot(
            outer_ref[...], jnp.concatenate([high, low, high], axis=0), preferred_element_type=F32
        ).astype(BF16)
        out_ref[0, 2 * pair] = lags[:, :128]
        out_ref[0, 2 * pair + 1] = lags[:, 128:]


def vmem():
    return pl.BlockSpec(memory_space=pltpu.VMEM)


def local(traces, pair_blocks, pair_counts):
    stations, segs, length = traces.shape
    rows = traces.reshape(stations, segs, 32, 128).transpose(0, 2, 1, 3).reshape(1024, 128)
    white, need = pl.pallas_call(
        whiten_kernel,
        out_shape=(
            jax.ShapeDtypeStruct((NY, CHUNKS, 4, 16, 128), BF16),
            jax.ShapeDtypeStruct((8, 128), jnp.int32),
        ),
        in_specs=[vmem()] * 6,
        out_specs=(vmem(), vmem()),
        compiler_params=pltpu.CompilerParams(vmem_limit_bytes=32 * MIB),
        name="whiten",
    )(rows, pair_blocks, *forward_tables())
    dma = pltpu.SemaphoreType.DMA
    stacked = pl.pallas_call(
        exchange_kernel,
        out_shape=jax.ShapeDtypeStruct((NY, CHUNKS, 8, 32, 128), BF16),
        in_specs=[vmem(), vmem(), pl.BlockSpec(memory_space=pltpu.SMEM)],
        out_specs=pl.BlockSpec(memory_space=pl.ANY),
        scratch_shapes=[
            *[pltpu.VMEM((NZ, NY, 4, 16, 128), BF16)] * RINGS,
            *[pltpu.VMEM((2 * NX, NZ, NY, 16, 128), BF16)] * CHUNKS,
            pltpu.VMEM((NZ, NX, NY, 4, 16, 128), BF16),
            pltpu.VMEM((CHUNKS, 2 * NX, NZ, NY, 16, 128), BF16),
            pltpu.VMEM((RINGS, 2, NZ, NY, 16, 128), BF16),
            pltpu.VMEM((4, 2, 4, 8, 8, 128), F32),
            pltpu.VMEM((CHUNKS, SLOTS, 32, 128), BF16),
            pltpu.VMEM((2 * NX, 8, 128), jnp.int32),
            pltpu.SMEM((2 * NX, 8, 128), jnp.int32),
            dma((2 * NX, 2)),
            dma(()),
            dma((CHUNKS,)),
            dma((CHUNKS, NY, 2)),
            dma((RINGS, NZ, 2)),
            dma((RINGS, 9, 2)),
            dma((16, 2)),
            dma((CHUNKS, NY, 2)),
            dma((CHUNKS,)),
        ],
        compiler_params=pltpu.CompilerParams(
            collective_id=0, has_side_effects=True, vmem_limit_bytes=40 * MIB
        ),
        name="exchange",
    )(white, need, pair_blocks)
    whole = lambda *shape: pl.BlockSpec(shape, lambda p: (0,) * len(shape))
    lags = pl.pallas_call(
        invert_kernel,
        out_shape=jax.ShapeDtypeStruct((8, 4, 128, 128), BF16),
        grid=(8,),
        in_specs=[
            pl.BlockSpec(memory_space=pltpu.SMEM),
            pl.BlockSpec((NY, CHUNKS, 1, 32, 128), lambda p: (0, 0, p, 0, 0)),
            whole(256, 256),
            whole(16, 8, 128),
            whole(16, 8, 128),
            whole(128, 768),
            whole(32, 128),
        ],
        out_specs=pl.BlockSpec((1, 4, 128, 128), lambda p: (p, 0, 0, 0)),
        compiler_params=pltpu.CompilerParams(vmem_limit_bytes=32 * MIB),
        name="invert",
    )(pair_counts, stacked, *inverse_tables())
    return lags.reshape(8, 4, 32, 4, 128).transpose(0, 1, 3, 2, 4).reshape(8, 4, 4, length)


def solution(mesh):
    in_specs = (P("sta", "seg", None), P("sta", None), P("sta"))
    out_specs = P(("sta", "seg"), None, None, None)
    return jax.shard_map(local, mesh=mesh, in_specs=in_specs, out_specs=out_specs, check_vma=False)
```

```python
import functools
import math

import jax
import jax.numpy as jnp
import ml_dtypes
import numpy as np
from jax import lax
from jax.experimental import pallas as pl
from jax.experimental.pallas import tpu as pltpu
from jax.sharding import PartitionSpec as P

MESH = pl.DeviceIdType.MESH
F32 = jnp.float32
BF16 = jnp.bfloat16
HIGHEST = lax.Precision.HIGHEST
EPSILON = 1e-06
NX, NZ, NY = 4, 8, 4
CHUNKS = 4
RINGS = 3
ORDER = (0, 3, 1, 2)
PLACES = (0, 1, 7, 2, 6, 3, 5, 4)
NEAR = 5
UNROLL = 2
SLOTS = 32
STEP = 4
MIB = 1 << 20


def split_high(table):
    high = table.astype(ml_dtypes.bfloat16)
    return high, (table - high.astype(np.float64)).astype(ml_dtypes.bfloat16)


def forward_tables():
    a = np.arange(32)
    outer = np.zeros((2, 16, 2, 4, 2, 4, 32, 2))
    for c in range(16):
        for e in range(2):
            angle = 2 * np.pi * (a * (2 * c + e) % 32) / 32
            for g in range(2):
                for j in range(4):
                    outer[0, c, g, j, e, j, :, g] = np.cos(angle)
                    outer[1, c, g, j, e, j, :, g] = -np.sin(angle)
    k = np.broadcast_to(2 * np.arange(16)[:, None, None] + np.arange(2), (16, 8, 2)).reshape(256)
    twist = 2 * np.pi * (k[:, None] * np.arange(128)) / 4096
    inner = 2 * np.pi * (np.arange(128)[:, None] * np.arange(64) % 128) / 128
    cos, sin = np.cos(inner), np.sin(inner)
    inner = np.concatenate([np.concatenate([cos, -sin], 1), np.concatenate([sin, cos], 1)], 0)
    return tuple(
        t.astype(np.float32) for t in (outer.reshape(512, 256), np.cos(twist), np.sin(twist), inner)
    )


def inverse_tables():
    inner = 2 * np.pi * (np.arange(64)[:, None] * np.arange(128) % 128) / 128
    cos, sin = np.cos(inner) / 64, np.sin(inner) / 64
    inner = np.concatenate([np.concatenate([cos, sin], 1), np.concatenate([-sin, cos], 1)], 0)
    inner = np.concatenate(split_high(inner), 0)
    k = np.broadcast_to(2 * np.arange(16)[:, None, None] + np.arange(2), (16, 4, 2)).reshape(16, 8)
    twist = 2 * np.pi * (k[:, :, None] * np.arange(128)) / 4096
    outer = np.zeros((32, 4, 2, 16, 4, 2))
    u = np.arange(32)
    for c in range(16):
        for e in range(2):
            angle = 2 * np.pi * (u * (2 * c + e) % 32) / 32
            for j in range(4):
                outer[:, j, 0, c, j, e] = np.cos(angle)
                outer[:, j, 1, c, j, e] = -np.sin(angle)
    high, low = split_high(outer.reshape(128, 256))
    outer = np.concatenate([high, high, low], 1)
    weight = np.ones((32, 128))
    weight[::2, 0] = 0.5
    return (
        inner,
        np.cos(twist).astype(np.float32),
        np.sin(twist).astype(np.float32),
        outer,
        weight.astype(ml_dtypes.bfloat16),
    )


def whiten(x_ref, outer_ref, cos_ref, sin_ref, inner_ref, white_ref):
    x = x_ref[...].reshape(16, 8, 8, 128)
    total = jnp.sum(x, axis=1)
    total = total + pltpu.roll(total, 4, 1)
    total = total + pltpu.roll(total, 2, 1)
    mean = jnp.sum(total, axis=-1, keepdims=True) * (1.0 / 4096)
    x = (x - mean[:, None]).reshape(4, 256, 128)
    row = lax.broadcasted_iota(jnp.int32, (2, 8, 128), 1)
    lane = lax.broadcasted_iota(jnp.int32, (2, 8, 128), 2)
    for half in range(2):
        both = jnp.concatenate([x[2 * half], x[2 * half + 1]], axis=1)
        section = jnp.dot(outer_ref[...], both, precision=HIGHEST, preferred_element_type=F32)
        cos, sin = cos_ref[...], sin_ref[...]
        for b in range(2):
            real = section[:256, 128 * b : 128 * b + 128]
            imag = section[256:, 128 * b : 128 * b + 128]
            turned = jnp.concatenate([real * cos + imag * sin, imag * cos - real * sin], axis=1)
            spec = jnp.dot(turned, inner_ref[...], precision=HIGHEST, preferred_element_type=F32)
            spec = spec.reshape(16, 2, 8, 128)
            power = jnp.sum(spec * spec, axis=0)
            power = power + jnp.where(row % 2 == 0, pltpu.roll(power, 7, 1), pltpu.roll(power, 1, 1))
            power = power + jnp.where(lane % 2 == 0, pltpu.roll(power, 127, 2), pltpu.roll(power, 1, 2))
            power = power + pltpu.roll(power, 64, 2)
            white = spec * (1.0 / jnp.sqrt(power * (1.0 / 64) + EPSILON))
            white_ref[:, :, 2 * half + b] = white.reshape(4, 4, 16, 128).astype(BF16)


def blocks_named(partner):
    row = lax.broadcasted_iota(jnp.int32, (SLOTS, SLOTS), 0)
    column = lax.broadcasted_iota(jnp.int32, (SLOTS, SLOTS), 1)
    partner = jnp.sum(jnp.where(row == column, partner, 0), axis=1, keepdims=True)
    source = lax.broadcasted_iota(jnp.int32, (SLOTS, 128), 1)
    named = jnp.sum(jnp.where(partner // 4 == source, partner % 4, 0), axis=0, keepdims=True)
    return jnp.broadcast_to(named, (8, 128))


def exchange_kernel(
    rows_ref, outer_ref, cos_ref, sin_ref, inner_ref, partners_ref, pairs_ref, stacked_ref, *scratch
):
    chosen, rings = scratch[:CHUNKS], scratch[CHUNKS : CHUNKS + RINGS + 1]
    near, far = rings[:2]
    load, scratch = scratch[CHUNKS + RINGS + 1 : CHUNKS + RINGS + 6], scratch[CHUNKS + RINGS + 6 :]
    white_ref, need_ref, group, picked, bounce, sides, cross, table, lookup = scratch[:9]
    load_sem, need_sem, table_sem, own_sem, y_sem, z_sem, x_sem, g_sem, c_sem, keep_sem = scratch[9:]
    sta, q = lax.axis_index("sta"), lax.axis_index("seg")
    x, z, core = sta // 16, sta // 2 % 8, sta % 2

    def at(dx, dz, flip):
        other = core if flip == 0 else 1 - core
        return (((x + dx) % NX * NZ + (z + dz) % NZ) * 2 + other, q)

    def along(dy):
        return (sta, (q + dy) % NY)

    row_peers = [(d, f) for d in range(NX) for f in range(2) if (d, f) != (0, 0)]
    up, down, right, left = at(0, 1, 0), at(0, NZ - 1, 0), at(1, 0, 0), at(NX - 1, 0, 0)
    targets = [along(r) for r in range(1, NY)] + [up, down] + [at(d, 0, f) for d, f in row_peers]
    barrier = pltpu.get_barrier_semaphore()
    for target in targets:
        pl.semaphore_signal(barrier, inc=1, device_id=target, device_id_type=MESH)
    loads = [
        pltpu.make_async_copy(source, target, load_sem.at[i])
        for i, (source, target) in enumerate(zip((rows_ref, outer_ref, cos_ref, sin_ref, inner_ref), load))
    ]
    for copy in loads:
        copy.start()
    need_ref[...] = blocks_named(partners_ref[1:2])
    table[0] = need_ref[...]
    for copy in loads:
        copy.wait()
    whiten(*load, white_ref)
    pl.semaphore_wait(barrier, len(targets))

    started = []

    def send(source, destination, sems, target):
        copy = pltpu.make_async_remote_copy(
            source, destination, sems.at[0], sems.at[1], device_id=target, device_id_type=MESH
        )
        copy.start()
        started.append(copy)
        return copy

    def ring(c, dz):
        place = PLACES.index(dz)
        if c:
            return rings[c + 1].at[place]
        return near.at[place] if place < NEAR else far.at[place - NEAR]

    def home(c):
        return ring(c, 0) if c < RINGS else group.at[0, 0]

    own, y_in = {}, {}
    for c in ORDER:
        y_in[c] = [
            send(white_ref.at[(q + r) % NY, c], home(c).at[r], y_sem.at[c, r], along(r)) for r in range(1, NY)
        ]
        own[c] = pltpu.make_async_copy(white_ref.at[q, c], home(c).at[0], own_sem.at[c])
        own[c].start()
    need_in = [
        send(need_ref, table.at[d * 2 + f], need_sem.at[d * 2 + f], at(d, 0, f)) for d, f in row_peers
    ]

    def home_ready(c):
        own[c].wait()
        for copy in y_in[c]:
            copy.wait_recv()

    def landed(copies):
        for copy in copies:
            copy.wait_recv()

    hops = {}

    def hop(c, t):
        if t == 1:
            home_ready(c)
        else:
            landed(hops[c, t - 1])
        hops[c, t] = []
        if t < 4 or c % 2 == 0:
            hops[c, t].append(send(ring(c, t - 1), ring(c, t), z_sem.at[c, t], up))
        if t < 4 or c % 2 == 1:
            hops[c, t].append(send(ring(c, (9 - t) % 8), ring(c, 8 - t), z_sem.at[c, 8 - t], down))

    def pick(c, part):
        def one(slot, carry):
            for place in range(*part):
                dz = PLACES[place]
                block = lookup[slot, 0, (x * NZ + (z - dz) % NZ) * 2 + core]
                picked[c, slot, place] = ring(c, dz)[:, block]
            return carry

        if part[1] == NZ:
            landed(hops[c, 4])
        lax.fori_loop(0, 2 * NX, one, 0)
        chosen[c][0, part[0] : part[1]] = picked[c, 0, part[0] : part[1]]

    arrivals, relays = {c: [] for c in range(CHUNKS)}, {}

    def spread(c, part):
        some = slice(*part)
        sems = x_sem.at[c, int(part[0] > 0)]

        def pass_on(slot, target, sem, device):
            return send(picked.at[c, slot, some], target.at[some], sems.at[sem], device)

        relays[c, part] = [
            pass_on(4, bounce.at[c, 0], 0, right),
            pass_on(5, bounce.at[c, 1], 1, left),
        ]
        arrivals[c] += [
            pass_on(6, chosen[c].at[2], 2, right),
            pass_on(2, chosen[c].at[6], 3, left),
            pass_on(7, chosen[c].at[3], 4, at(1, 0, 1)),
            pass_on(3, chosen[c].at[7], 5, at(NX - 1, 0, 1)),
            pass_on(1, chosen[c].at[1], 6, at(0, 0, 1)),
        ]

    def forward(c, part):
        some = slice(*part)
        sems = x_sem.at[c, int(part[0] > 0)]
        relays[c, part][0].wait_recv()
        arrivals[c].append(send(bounce.at[c, 0, some], chosen[c].at[4, some], sems.at[7], right))
        relays[c, part][1].wait_recv()
        arrivals[c].append(send(bounce.at[c, 1, some], chosen[c].at[5, some], sems.at[8], at(NX - 1, 0, 1)))

    last = CHUNKS - 1
    steps = {}

    def group_start():
        home_ready(last)
        steps["x"] = [
            send(group.at[0, 0], group.at[0, 1], g_sem.at[0], right),
            send(group.at[0, 0], group.at[0, 3], g_sem.at[1], left),
        ]

    def group_across():
        steps["x"][0].wait_recv()
        one = send(group.at[0, 1, 0:2], group.at[0, 2, 0:2], g_sem.at[2], right)
        steps["x"][1].wait_recv()
        steps[0] = [one, send(group.at[0, 3, 2:4], group.at[0, 2, 2:4], g_sem.at[3], left)]

    def group_hop(t):
        landed(steps[t - 1])
        if t < 4:
            parts = (slice(0, 4), slice(0, 4))
        else:
            parts = (slice(0, 2), slice(2, 4))
        steps[t] = [
            send(group.at[t - 1, parts[0]], group.at[t, parts[0]], g_sem.at[2 * t + 2], up),
            send(group.at[(9 - t) % 8, parts[1]], group.at[8 - t, parts[1]], g_sem.at[2 * t + 3], down),
        ]

    def group_pick():
        def one(dx, carry):
            for place, dz in enumerate(PLACES):
                source = ((x - dx) % NX * NZ + (z - dz) % NZ) * 2 + core
                picked[last, dx, place] = group[dz, dx, :, lookup[1, 0, source]]
                chosen[last][dx * 2, place] = group[dz, dx, :, lookup[0, 0, source]]
            return carry

        landed(steps[4])
        lax.fori_loop(0, NX, one, 0)
        arrivals[last] += [
            send(picked.at[last, d], chosen[last].at[2 * d + 1], g_sem.at[12 + d], at(0, 0, 1)) for d in range(NX)
        ]

    row = lax.broadcasted_iota(jnp.int32, (8, 128), 0)
    first_half = lax.broadcasted_iota(jnp.int32, (8, 128), 1) < 64

    def prepare(c):
        def one(step, carry):
            b, r = step // NY, step % NY
            both = home(c)[r, b].astype(F32)
            for g in range(2):
                value = both[8 * g : 8 * g + 8]
                turned = pltpu.roll(value, 64, 1)
                for part, side in enumerate(
                    (jnp.where(first_half, value, -turned), jnp.where(first_half, turned, value))
                ):
                    for i in range(4):
                        only = jnp.where(row // 2 == i, side, 0.0)
                        only = only + pltpu.roll(only, 2, 0)
                        sides[side_of(c), b, part, i, r * 2 + g] = only + pltpu.roll(only, 4, 0)
            return carry

        lax.fori_loop(0, 4 * NY, one, 0)

    kept, handed = [], []

    def side_of(c):
        return int(c in (1, 2))

    def multiply(c):
        landed(arrivals[c])
        for r in (2, 1, 3, 0):
            base = (q + r) % NY * 8

            def one(n, carry):
                slot = base + n
                first = pairs_ref[0, slot] % 4
                partner = pairs_ref[1, slot] // 4
                dx, dz, flip = (x - partner // 16) % NX, (z - partner // 2 % 8) % NZ, (core + partner) % 2
                place = jnp.where(dz == 0, 0, jnp.where(dz <= 4, 2 * dz - 1, 2 * (NZ - dz)))
                second = chosen[c][dx * 2 + flip, place].astype(F32)
                rows = []
                for i in range(4):
                    straight = sides[side_of(c), first, 0, i, 0] * second[0, 0:8]
                    crossed = sides[side_of(c), first, 1, i, 0] * second[0, 0:8]
                    for g in range(1, 8):
                        part = second[g // 2, 8 * (g % 2) : 8 * (g % 2) + 8]
                        straight = straight + sides[side_of(c), first, 0, i, g] * part
                        crossed = crossed + sides[side_of(c), first, 1, i, g] * part
                    rows.append(straight + pltpu.roll(crossed, 64, 1))
                cross[c, slot] = jnp.concatenate(rows, axis=0).astype(BF16)
                return carry

            lax.fori_loop(0, 8, one, 0, unroll=UNROLL)
            part = cross.at[c, pl.ds(base, 8)]
            if r:
                handed.append(send(part, stacked_ref.at[q, c], c_sem.at[c, r], along(r)))
            else:
                copy = pltpu.make_async_copy(part, stacked_ref.at[q, c], keep_sem.at[c])
                copy.start()
                kept.append(copy)

    near_part, far_part, whole = (0, NEAR), (NEAR, NZ), (0, NZ)
    hop(0, 1)
    group_start()
    hop(1, 1)
    hop(0, 2)
    landed(need_in)
    copy = pltpu.make_async_copy(table, lookup, table_sem)
    copy.start()
    copy.wait()
    group_across()
    hop(2, 1)
    hop(1, 2)
    hop(0, 3)
    pick(0, near_part)
    spread(0, near_part)
    hop(2, 2)
    hop(1, 3)
    hop(0, 4)
    group_hop(1)
    pick(0, far_part)
    forward(0, near_part)
    spread(0, far_part)
    hop(2, 3)
    hop(1, 4)
    pick(1, whole)
    forward(0, far_part)
    spread(1, whole)
    hop(2, 4)
    group_hop(2)
    prepare(0)
    pick(2, whole)
    multiply(0)
    forward(1, whole)
    spread(2, whole)
    group_hop(3)
    prepare(1)
    prepare(last)
    multiply(1)
    group_hop(4)
    prepare(2)
    forward(2, whole)
    group_pick()
    multiply(last)
    multiply(2)
    for copy in kept:
        copy.wait()
    landed(handed)
    for copy in started:
        copy.wait_send()


def invert_kernel(counts_ref, stacked_ref, inner_ref, cos_ref, sin_ref, outer_ref, weight_ref, out_ref):
    for n in range(STEP):
        slot = lax.axis_index("seg") * 8 + pl.program_id(0) * STEP + n
        live = (slot < counts_ref[0]).astype(F32)
        cross = stacked_ref[:, :, n].reshape(16, 32, 128)
        cross = jnp.concatenate([cross[0:1] * weight_ref[...], cross[1:]], axis=0).reshape(512, 128)
        series = jnp.dot(jnp.concatenate([cross, cross], axis=1), inner_ref[...], preferred_element_type=F32)
        series = series.reshape(16, 4, 8, 256)
        cos, sin = cos_ref[...] * live, sin_ref[...] * live
        parts = []
        for i in range(4):
            real, imag = series[:, i, :, :128], series[:, i, :, 128:]
            turned = jnp.concatenate(
                [(real * cos - imag * sin).reshape(128, 128), (real * sin + imag * cos).reshape(128, 128)], axis=0
            )
            parts.append(turned)
        for pair in range(2):
            both = jnp.concatenate([parts[2 * pair], parts[2 * pair + 1]], axis=1)
            high = both.astype(BF16)
            low = (both - high.astype(F32)).astype(BF16)
            lags = jnp.dot(
                outer_ref[...], jnp.concatenate([high, low, high], axis=0), preferred_element_type=F32
            ).astype(BF16)
            out_ref[n, 2 * pair] = lags[:, :128]
            out_ref[n, 2 * pair + 1] = lags[:, 128:]


def vmem():
    return pl.BlockSpec(memory_space=pltpu.VMEM)


def local(traces, pair_blocks, pair_counts):
    stations, segs, length = traces.shape
    rows = traces.reshape(stations, segs, 32, 128).transpose(0, 2, 1, 3).reshape(1024, 128)
    dma = pltpu.SemaphoreType.DMA
    smem = pl.BlockSpec(memory_space=pltpu.SMEM)
    stacked = pl.pallas_call(
        exchange_kernel,
        out_shape=jax.ShapeDtypeStruct((NY, CHUNKS, 8, 32, 128), BF16),
        in_specs=[pl.BlockSpec(memory_space=pltpu.HBM)] * 5 + [vmem(), smem],
        out_specs=pl.BlockSpec(memory_space=pl.ANY),
        scratch_shapes=[
            *[pltpu.VMEM((2 * NX, NZ, NY, 16, 128), BF16)] * CHUNKS,
            pltpu.VMEM((NEAR, NY, 4, 16, 128), BF16),
            pltpu.VMEM((NZ - NEAR, NY, 4, 16, 128), BF16),
            *[pltpu.VMEM((NZ, NY, 4, 16, 128), BF16)] * (RINGS - 1),
            pltpu.VMEM((1024, 128), F32),
            pltpu.VMEM((512, 256), F32),
            pltpu.VMEM((256, 128), F32),
            pltpu.VMEM((256, 128), F32),
            pltpu.VMEM((256, 128), F32),
            pltpu.VMEM((NY, CHUNKS, 4, 16, 128), BF16),
            pltpu.VMEM((8, 128), jnp.int32),
            pltpu.VMEM((NZ, NX, NY, 4, 16, 128), BF16),
            pltpu.VMEM((CHUNKS, 2 * NX, NZ, NY, 16, 128), BF16),
            pltpu.VMEM((RINGS, 2, NZ, NY, 16, 128), BF16),
            pltpu.VMEM((2, 4, 2, 4, 8, 8, 128), F32),
            pltpu.VMEM((CHUNKS, SLOTS, 32, 128), BF16),
            pltpu.VMEM((2 * NX, 8, 128), jnp.int32),
            pltpu.SMEM((2 * NX, 8, 128), jnp.int32),
            dma((5,)),
            dma((2 * NX, 2)),
            dma(()),
            dma((CHUNKS,)),
            dma((CHUNKS, NY, 2)),
            dma((RINGS, NZ, 2)),
            dma((RINGS, 2, 9, 2)),
            dma((16, 2)),
            dma((CHUNKS, NY, 2)),
            dma((CHUNKS,)),
        ],
        compiler_params=pltpu.CompilerParams(
            collective_id=0, has_side_effects=True, vmem_limit_bytes=63 * MIB
        ),
        name="exchange",
    )(rows, *forward_tables(), pair_blocks.T, pair_blocks.T)
    whole = lambda *shape: pl.BlockSpec(shape, lambda p: (0,) * len(shape))
    lags = pl.pallas_call(
        invert_kernel,
        out_shape=jax.ShapeDtypeStruct((8, 4, 128, 128), BF16),
        grid=(8 // STEP,),
        in_specs=[
            smem,
            pl.BlockSpec((NY, CHUNKS, STEP, 32, 128), lambda p: (0, 0, p, 0, 0)),
            whole(256, 256),
            whole(16, 8, 128),
            whole(16, 8, 128),
            whole(128, 768),
            whole(32, 128),
        ],
        out_specs=pl.BlockSpec((STEP, 4, 128, 128), lambda p: (p, 0, 0, 0)),
        compiler_params=pltpu.CompilerParams(vmem_limit_bytes=32 * MIB),
        name="invert",
    )(pair_counts, stacked, *inverse_tables())
    return lags.reshape(8, 4, 32, 4, 128).transpose(0, 1, 3, 2, 4).reshape(8, 4, 4, length)


def solution(mesh):
    in_specs = (P("sta", "seg", None), P("sta", None), P("sta"))
    out_specs = P(("sta", "seg"), None, None, None)
    return jax.shard_map(local, mesh=mesh, in_specs=in_specs, out_specs=out_specs, check_vma=False)
```

```python
import functools
import math

import jax
import jax.numpy as jnp
import ml_dtypes
import numpy as np
from jax import lax
from jax.experimental import pallas as pl
from jax.experimental.pallas import tpu as pltpu
from jax.sharding import PartitionSpec as P

MESH = pl.DeviceIdType.MESH
F32 = jnp.float32
BF16 = jnp.bfloat16
HIGHEST = lax.Precision.HIGHEST
EPSILON = 1e-06
NX, NZ, NY = 4, 8, 4
CHUNKS = 4
RINGS = 3
ORDER = (0, 3, 1, 2)
PLACES = (0, 1, 7, 2, 6, 3, 5, 4)
NEAR = 5
UNROLL = 4
SLOTS = 32
STEP = 2
MIB = 1 << 20


def split_high(table):
    high = table.astype(ml_dtypes.bfloat16)
    return high, (table - high.astype(np.float64)).astype(ml_dtypes.bfloat16)


def forward_tables():
    a = np.arange(32)
    outer = np.zeros((2, 16, 2, 4, 2, 4, 32, 2))
    for c in range(16):
        for e in range(2):
            angle = 2 * np.pi * (a * (2 * c + e) % 32) / 32
            for g in range(2):
                for j in range(4):
                    outer[0, c, g, j, e, j, :, g] = np.cos(angle)
                    outer[1, c, g, j, e, j, :, g] = -np.sin(angle)
    k = np.broadcast_to(2 * np.arange(16)[:, None, None] + np.arange(2), (16, 8, 2)).reshape(256)
    twist = 2 * np.pi * (k[:, None] * np.arange(128)) / 4096
    inner = 2 * np.pi * (np.arange(128)[:, None] * np.arange(64) % 128) / 128
    cos, sin = np.cos(inner), np.sin(inner)
    inner = np.concatenate([np.concatenate([cos, -sin], 1), np.concatenate([sin, cos], 1)], 0)
    return tuple(
        t.astype(np.float32) for t in (outer.reshape(512, 256), np.cos(twist), np.sin(twist), inner)
    )


def inverse_tables():
    inner = 2 * np.pi * (np.arange(64)[:, None] * np.arange(128) % 128) / 128
    cos, sin = np.cos(inner) / 64, np.sin(inner) / 64
    inner = np.concatenate([np.concatenate([cos, sin], 1), np.concatenate([-sin, cos], 1)], 0)
    inner = np.concatenate(split_high(inner), 0)
    k = np.broadcast_to(2 * np.arange(16)[:, None, None] + np.arange(2), (16, 4, 2)).reshape(16, 8)
    twist = 2 * np.pi * (k[:, :, None] * np.arange(128)) / 4096
    outer = np.zeros((32, 4, 2, 16, 4, 2))
    u = np.arange(32)
    for c in range(16):
        for e in range(2):
            angle = 2 * np.pi * (u * (2 * c + e) % 32) / 32
            for j in range(4):
                outer[:, j, 0, c, j, e] = np.cos(angle)
                outer[:, j, 1, c, j, e] = -np.sin(angle)
    high, low = split_high(outer.reshape(128, 256))
    outer = np.concatenate([high, high, low], 1)
    weight = np.ones((32, 128))
    weight[::2, 0] = 0.5
    return (
        inner,
        np.cos(twist).astype(np.float32),
        np.sin(twist).astype(np.float32),
        outer,
        weight.astype(ml_dtypes.bfloat16),
    )


def whiten(x_ref, outer_ref, cos_ref, sin_ref, inner_ref, white_ref):
    x = x_ref[...].reshape(16, 8, 8, 128)
    total = jnp.sum(x, axis=1)
    total = total + pltpu.roll(total, 4, 1)
    total = total + pltpu.roll(total, 2, 1)
    mean = jnp.sum(total, axis=-1, keepdims=True) * (1.0 / 4096)
    x = (x - mean[:, None]).reshape(4, 256, 128)
    row = lax.broadcasted_iota(jnp.int32, (2, 8, 128), 1)
    lane = lax.broadcasted_iota(jnp.int32, (2, 8, 128), 2)
    for half in range(2):
        both = jnp.concatenate([x[2 * half], x[2 * half + 1]], axis=1)
        section = jnp.dot(outer_ref[...], both, precision=HIGHEST, preferred_element_type=F32)
        cos, sin = cos_ref[...], sin_ref[...]
        for b in range(2):
            real = section[:256, 128 * b : 128 * b + 128]
            imag = section[256:, 128 * b : 128 * b + 128]
            turned = jnp.concatenate([real * cos + imag * sin, imag * cos - real * sin], axis=1)
            spec = jnp.dot(turned, inner_ref[...], precision=HIGHEST, preferred_element_type=F32)
            spec = spec.reshape(16, 2, 8, 128)
            power = jnp.sum(spec * spec, axis=0)
            power = power + jnp.where(row % 2 == 0, pltpu.roll(power, 7, 1), pltpu.roll(power, 1, 1))
            power = power + jnp.where(lane % 2 == 0, pltpu.roll(power, 127, 2), pltpu.roll(power, 1, 2))
            power = power + pltpu.roll(power, 64, 2)
            white = spec * (1.0 / jnp.sqrt(power * (1.0 / 64) + EPSILON))
            white_ref[:, :, 2 * half + b] = white.reshape(4, 4, 16, 128).astype(BF16)


def blocks_named(partner):
    row = lax.broadcasted_iota(jnp.int32, (SLOTS, SLOTS), 0)
    column = lax.broadcasted_iota(jnp.int32, (SLOTS, SLOTS), 1)
    partner = jnp.sum(jnp.where(row == column, partner, 0), axis=1, keepdims=True)
    source = lax.broadcasted_iota(jnp.int32, (SLOTS, 128), 1)
    named = jnp.sum(jnp.where(partner // 4 == source, partner % 4, 0), axis=0, keepdims=True)
    return jnp.broadcast_to(named, (8, 128))


def exchange_kernel(
    rows_ref, outer_ref, cos_ref, sin_ref, inner_ref, partners_ref, pairs_ref, stacked_ref, *scratch
):
    chosen, rings = scratch[:CHUNKS], scratch[CHUNKS : CHUNKS + RINGS + 1]
    near, far = rings[:2]
    load, scratch = scratch[CHUNKS + RINGS + 1 : CHUNKS + RINGS + 6], scratch[CHUNKS + RINGS + 6 :]
    white_ref, need_ref, group, picked, bounce, sides, cross, table, lookup = scratch[:9]
    load_sem, need_sem, table_sem, own_sem, y_sem, z_sem, x_sem, g_sem, c_sem, keep_sem = scratch[9:]
    sta, q = lax.axis_index("sta"), lax.axis_index("seg")
    x, z, core = sta // 16, sta // 2 % 8, sta % 2

    def at(dx, dz, flip):
        other = core if flip == 0 else 1 - core
        return (((x + dx) % NX * NZ + (z + dz) % NZ) * 2 + other, q)

    def along(dy):
        return (sta, (q + dy) % NY)

    row_peers = [(d, f) for d in range(NX) for f in range(2) if (d, f) != (0, 0)]
    up, down, right, left = at(0, 1, 0), at(0, NZ - 1, 0), at(1, 0, 0), at(NX - 1, 0, 0)
    targets = [along(r) for r in range(1, NY)] + [up, down] + [at(d, 0, f) for d, f in row_peers]
    barrier = pltpu.get_barrier_semaphore()
    for target in targets:
        pl.semaphore_signal(barrier, inc=1, device_id=target, device_id_type=MESH)
    loads = [
        pltpu.make_async_copy(source, target, load_sem.at[i])
        for i, (source, target) in enumerate(zip((rows_ref, outer_ref, cos_ref, sin_ref, inner_ref), load))
    ]
    for copy in loads:
        copy.start()
    need_ref[...] = blocks_named(partners_ref[1:2])
    table[0] = need_ref[...]
    for copy in loads:
        copy.wait()
    whiten(*load, white_ref)
    pl.semaphore_wait(barrier, len(targets))

    started = []

    def send(source, destination, sems, target):
        copy = pltpu.make_async_remote_copy(
            source, destination, sems.at[0], sems.at[1], device_id=target, device_id_type=MESH
        )
        copy.start()
        started.append(copy)
        return copy

    def ring(c, dz):
        place = PLACES.index(dz)
        if c:
            return rings[c + 1].at[place]
        return near.at[place] if place < NEAR else far.at[place - NEAR]

    def home(c):
        return ring(c, 0) if c < RINGS else group.at[0, 0]

    own, y_in = {}, {}
    for c in ORDER:
        y_in[c] = [
            send(white_ref.at[(q + r) % NY, c], home(c).at[r], y_sem.at[c, r], along(r)) for r in range(1, NY)
        ]
        own[c] = pltpu.make_async_copy(white_ref.at[q, c], home(c).at[0], own_sem.at[c])
        own[c].start()
    need_in = [
        send(need_ref, table.at[d * 2 + f], need_sem.at[d * 2 + f], at(d, 0, f)) for d, f in row_peers
    ]

    def home_ready(c):
        own[c].wait()
        for copy in y_in[c]:
            copy.wait_recv()

    def landed(copies):
        for copy in copies:
            copy.wait_recv()

    hops = {}

    def hop(c, t):
        if t == 1:
            home_ready(c)
        else:
            landed(hops[c, t - 1])
        hops[c, t] = []
        if t < 4 or c % 2 == 0:
            hops[c, t].append(send(ring(c, t - 1), ring(c, t), z_sem.at[c, t], up))
        if t < 4 or c % 2 == 1:
            hops[c, t].append(send(ring(c, (9 - t) % 8), ring(c, 8 - t), z_sem.at[c, 8 - t], down))

    def pick(c, part):
        def one(slot, carry):
            for place in range(*part):
                dz = PLACES[place]
                block = lookup[slot, 0, (x * NZ + (z - dz) % NZ) * 2 + core]
                picked[c, slot, place] = ring(c, dz)[:, block]
            return carry

        if part[1] == NZ:
            landed(hops[c, 4])
        lax.fori_loop(0, 2 * NX, one, 0)
        chosen[c][0, part[0] : part[1]] = picked[c, 0, part[0] : part[1]]

    arrivals, relays = {c: [] for c in range(CHUNKS)}, {}

    def spread(c, part):
        some = slice(*part)
        sems = x_sem.at[c, int(part[0] > 0)]

        def pass_on(slot, target, sem, device):
            return send(picked.at[c, slot, some], target.at[some], sems.at[sem], device)

        relays[c, part] = [
            pass_on(4, bounce.at[c, 0], 0, right),
            pass_on(5, bounce.at[c, 1], 1, left),
        ]
        arrivals[c] += [
            pass_on(6, chosen[c].at[2], 2, right),
            pass_on(2, chosen[c].at[6], 3, left),
            pass_on(7, chosen[c].at[3], 4, at(1, 0, 1)),
            pass_on(3, chosen[c].at[7], 5, at(NX - 1, 0, 1)),
            pass_on(1, chosen[c].at[1], 6, at(0, 0, 1)),
        ]

    def forward(c, part):
        some = slice(*part)
        sems = x_sem.at[c, int(part[0] > 0)]
        relays[c, part][0].wait_recv()
        arrivals[c].append(send(bounce.at[c, 0, some], chosen[c].at[4, some], sems.at[7], right))
        relays[c, part][1].wait_recv()
        arrivals[c].append(send(bounce.at[c, 1, some], chosen[c].at[5, some], sems.at[8], at(NX - 1, 0, 1)))

    last = CHUNKS - 1
    steps = {}

    def group_start():
        home_ready(last)
        steps["x"] = [
            send(group.at[0, 0], group.at[0, 1], g_sem.at[0], right),
            send(group.at[0, 0], group.at[0, 3], g_sem.at[1], left),
        ]

    def group_across():
        steps["x"][0].wait_recv()
        one = send(group.at[0, 1, 0:2], group.at[0, 2, 0:2], g_sem.at[2], right)
        steps["x"][1].wait_recv()
        steps[0] = [one, send(group.at[0, 3, 2:4], group.at[0, 2, 2:4], g_sem.at[3], left)]

    def group_hop(t):
        landed(steps[t - 1])
        if t < 4:
            parts = (slice(0, 4), slice(0, 4))
        else:
            parts = (slice(0, 2), slice(2, 4))
        steps[t] = [
            send(group.at[t - 1, parts[0]], group.at[t, parts[0]], g_sem.at[2 * t + 2], up),
            send(group.at[(9 - t) % 8, parts[1]], group.at[8 - t, parts[1]], g_sem.at[2 * t + 3], down),
        ]

    def group_pick():
        def one(dx, carry):
            for place, dz in enumerate(PLACES):
                source = ((x - dx) % NX * NZ + (z - dz) % NZ) * 2 + core
                picked[last, dx, place] = group[dz, dx, :, lookup[1, 0, source]]
                chosen[last][dx * 2, place] = group[dz, dx, :, lookup[0, 0, source]]
            return carry

        landed(steps[4])
        lax.fori_loop(0, NX, one, 0)
        arrivals[last] += [
            send(picked.at[last, d], chosen[last].at[2 * d + 1], g_sem.at[12 + d], at(0, 0, 1)) for d in range(NX)
        ]

    row = lax.broadcasted_iota(jnp.int32, (8, 128), 0)
    first_half = lax.broadcasted_iota(jnp.int32, (8, 128), 1) < 64

    def prepare(c):
        def one(step, carry):
            b, r = step // NY, step % NY
            both = home(c)[r, b].astype(F32)
            for g in range(2):
                value = both[8 * g : 8 * g + 8]
                turned = pltpu.roll(value, 64, 1)
                for part, side in enumerate(
                    (jnp.where(first_half, value, -turned), jnp.where(first_half, turned, value))
                ):
                    for i in range(4):
                        only = jnp.where(row // 2 == i, side, 0.0)
                        only = only + pltpu.roll(only, 2, 0)
                        sides[side_of(c), b, part, i, r * 2 + g] = only + pltpu.roll(only, 4, 0)
            return carry

        lax.fori_loop(0, 4 * NY, one, 0)

    kept, handed = [], []

    def side_of(c):
        return int(c in (1, 2))

    def multiply(c):
        landed(arrivals[c])
        for r in (2, 1, 3, 0):
            base = (q + r) % NY * 8

            def one(n, carry):
                slot = base + n
                first = pairs_ref[0, slot] % 4
                partner = pairs_ref[1, slot] // 4
                dx, dz, flip = (x - partner // 16) % NX, (z - partner // 2 % 8) % NZ, (core + partner) % 2
                place = jnp.where(dz == 0, 0, jnp.where(dz <= 4, 2 * dz - 1, 2 * (NZ - dz)))
                second = chosen[c][dx * 2 + flip, place].astype(F32)
                rows = []
                for i in range(4):
                    straight = sides[side_of(c), first, 0, i, 0] * second[0, 0:8]
                    crossed = sides[side_of(c), first, 1, i, 0] * second[0, 0:8]
                    for g in range(1, 8):
                        part = second[g // 2, 8 * (g % 2) : 8 * (g % 2) + 8]
                        straight = straight + sides[side_of(c), first, 0, i, g] * part
                        crossed = crossed + sides[side_of(c), first, 1, i, g] * part
                    rows.append(straight + pltpu.roll(crossed, 64, 1))
                cross[c, slot] = jnp.concatenate(rows, axis=0).astype(BF16)
                return carry

            lax.fori_loop(0, 8, one, 0, unroll=UNROLL)
            part = cross.at[c, pl.ds(base, 8)]
            if r:
                handed.append(send(part, stacked_ref.at[q, c], c_sem.at[c, r], along(r)))
            else:
                copy = pltpu.make_async_copy(part, stacked_ref.at[q, c], keep_sem.at[c])
                copy.start()
                kept.append(copy)

    near_part, far_part, whole = (0, NEAR), (NEAR, NZ), (0, NZ)
    hop(0, 1)
    group_start()
    hop(1, 1)
    hop(0, 2)
    landed(need_in)
    copy = pltpu.make_async_copy(table, lookup, table_sem)
    copy.start()
    copy.wait()
    group_across()
    hop(2, 1)
    hop(1, 2)
    hop(0, 3)
    pick(0, near_part)
    spread(0, near_part)
    hop(2, 2)
    hop(1, 3)
    hop(0, 4)
    group_hop(1)
    pick(0, far_part)
    forward(0, near_part)
    spread(0, far_part)
    hop(2, 3)
    hop(1, 4)
    pick(1, whole)
    forward(0, far_part)
    spread(1, whole)
    hop(2, 4)
    group_hop(2)
    prepare(0)
    pick(2, whole)
    group_hop(3)
    multiply(0)
    forward(1, whole)
    spread(2, whole)
    prepare(1)
    prepare(last)
    group_hop(4)
    multiply(1)
    forward(2, whole)
    group_pick()
    prepare(2)
    multiply(last)
    multiply(2)
    for copy in kept:
        copy.wait()
    landed(handed)
    for copy in started:
        copy.wait_send()


def invert_kernel(counts_ref, stacked_ref, inner_ref, cos_ref, sin_ref, outer_ref, weight_ref, out_ref):
    for n in range(STEP):
        slot = lax.axis_index("seg") * 8 + pl.program_id(0) * STEP + n
        live = (slot < counts_ref[0]).astype(F32)
        cross = stacked_ref[:, :, n].reshape(16, 32, 128)
        cross = jnp.concatenate([cross[0:1] * weight_ref[...], cross[1:]], axis=0).reshape(512, 128)
        series = jnp.dot(jnp.concatenate([cross, cross], axis=1), inner_ref[...], preferred_element_type=F32)
        series = series.reshape(16, 4, 8, 256)
        cos, sin = cos_ref[...] * live, sin_ref[...] * live
        parts = []
        for i in range(4):
            real, imag = series[:, i, :, :128], series[:, i, :, 128:]
            turned = jnp.concatenate(
                [(real * cos - imag * sin).reshape(128, 128), (real * sin + imag * cos).reshape(128, 128)], axis=0
            )
            parts.append(turned)
        for pair in range(2):
            both = jnp.concatenate([parts[2 * pair], parts[2 * pair + 1]], axis=1)
            high = both.astype(BF16)
            low = (both - high.astype(F32)).astype(BF16)
            lags = jnp.dot(
                outer_ref[...], jnp.concatenate([high, low, high], axis=0), preferred_element_type=F32
            ).astype(BF16)
            out_ref[n, 2 * pair] = lags[:, :128]
            out_ref[n, 2 * pair + 1] = lags[:, 128:]


def vmem():
    return pl.BlockSpec(memory_space=pltpu.VMEM)


def local(traces, pair_blocks, pair_counts):
    stations, segs, length = traces.shape
    rows = traces.reshape(stations, segs, 32, 128).transpose(0, 2, 1, 3).reshape(1024, 128)
    dma = pltpu.SemaphoreType.DMA
    smem = pl.BlockSpec(memory_space=pltpu.SMEM)
    stacked = pl.pallas_call(
        exchange_kernel,
        out_shape=jax.ShapeDtypeStruct((NY, CHUNKS, 8, 32, 128), BF16),
        in_specs=[pl.BlockSpec(memory_space=pltpu.HBM)] * 5 + [vmem(), smem],
        out_specs=pl.BlockSpec(memory_space=pl.ANY),
        scratch_shapes=[
            *[pltpu.VMEM((2 * NX, NZ, NY, 16, 128), BF16)] * CHUNKS,
            pltpu.VMEM((NEAR, NY, 4, 16, 128), BF16),
            pltpu.VMEM((NZ - NEAR, NY, 4, 16, 128), BF16),
            *[pltpu.VMEM((NZ, NY, 4, 16, 128), BF16)] * (RINGS - 1),
            pltpu.VMEM((1024, 128), F32),
            pltpu.VMEM((512, 256), F32),
            pltpu.VMEM((256, 128), F32),
            pltpu.VMEM((256, 128), F32),
            pltpu.VMEM((256, 128), F32),
            pltpu.VMEM((NY, CHUNKS, 4, 16, 128), BF16),
            pltpu.VMEM((8, 128), jnp.int32),
            pltpu.VMEM((NZ, NX, NY, 4, 16, 128), BF16),
            pltpu.VMEM((CHUNKS, 2 * NX, NZ, NY, 16, 128), BF16),
            pltpu.VMEM((RINGS, 2, NZ, NY, 16, 128), BF16),
            pltpu.VMEM((2, 4, 2, 4, 8, 8, 128), F32),
            pltpu.VMEM((CHUNKS, SLOTS, 32, 128), BF16),
            pltpu.VMEM((2 * NX, 8, 128), jnp.int32),
            pltpu.SMEM((2 * NX, 8, 128), jnp.int32),
            dma((5,)),
            dma((2 * NX, 2)),
            dma(()),
            dma((CHUNKS,)),
            dma((CHUNKS, NY, 2)),
            dma((RINGS, NZ, 2)),
            dma((RINGS, 2, 9, 2)),
            dma((16, 2)),
            dma((CHUNKS, NY, 2)),
            dma((CHUNKS,)),
        ],
        compiler_params=pltpu.CompilerParams(
            collective_id=0, has_side_effects=True, vmem_limit_bytes=60 * MIB
        ),
        name="exchange",
    )(rows, *forward_tables(), pair_blocks.T, pair_blocks.T)
    whole = lambda *shape: pl.BlockSpec(shape, lambda p: (0,) * len(shape))
    lags = pl.pallas_call(
        invert_kernel,
        out_shape=jax.ShapeDtypeStruct((8, 4, 128, 128), BF16),
        grid=(8 // STEP,),
        in_specs=[
            smem,
            pl.BlockSpec((NY, CHUNKS, STEP, 32, 128), lambda p: (0, 0, p, 0, 0)),
            whole(256, 256),
            whole(16, 8, 128),
            whole(16, 8, 128),
            whole(128, 768),
            whole(32, 128),
        ],
        out_specs=pl.BlockSpec((STEP, 4, 128, 128), lambda p: (p, 0, 0, 0)),
        compiler_params=pltpu.CompilerParams(vmem_limit_bytes=32 * MIB),
        name="invert",
    )(pair_counts, stacked, *inverse_tables())
    return lags.reshape(8, 4, 32, 4, 128).transpose(0, 1, 3, 2, 4).reshape(8, 4, 4, length)


def solution(mesh):
    in_specs = (P("sta", "seg", None), P("sta", None), P("sta"))
    out_specs = P(("sta", "seg"), None, None, None)
    return jax.shard_map(local, mesh=mesh, in_specs=in_specs, out_specs=out_specs, check_vma=False)
```

```python
import functools
import math

import jax
import jax.numpy as jnp
import ml_dtypes
import numpy as np
from jax import lax
from jax.experimental import pallas as pl
from jax.experimental.pallas import tpu as pltpu
from jax.sharding import PartitionSpec as P

MESH = pl.DeviceIdType.MESH
F32 = jnp.float32
BF16 = jnp.bfloat16
HIGHEST = lax.Precision.HIGHEST
EPSILON = 1e-06
NX, NZ, NY = 4, 8, 4
CHUNKS = 4
RINGS = 3
ORDER = (0, 3, 1, 2)
PLACES = (0, 1, 7, 2, 6, 3, 5, 4)
NEAR = 5
UNROLL = 4
SLOTS = 32
STEP = 2
MIB = 1 << 20


def split_high(table):
    high = table.astype(ml_dtypes.bfloat16)
    return high, (table - high.astype(np.float64)).astype(ml_dtypes.bfloat16)


def forward_tables():
    a = np.arange(32)
    outer = np.zeros((2, 16, 2, 4, 2, 4, 32, 2))
    for c in range(16):
        for e in range(2):
            angle = 2 * np.pi * (a * (2 * c + e) % 32) / 32
            for g in range(2):
                for j in range(4):
                    outer[0, c, g, j, e, j, :, g] = np.cos(angle)
                    outer[1, c, g, j, e, j, :, g] = -np.sin(angle)
    k = np.broadcast_to(2 * np.arange(16)[:, None, None] + np.arange(2), (16, 8, 2)).reshape(256)
    twist = 2 * np.pi * (k[:, None] * np.arange(128)) / 4096
    inner = 2 * np.pi * (np.arange(128)[:, None] * np.arange(64) % 128) / 128
    cos, sin = np.cos(inner), np.sin(inner)
    inner = np.concatenate([np.concatenate([cos, -sin], 1), np.concatenate([sin, cos], 1)], 0)
    return tuple(
        t.astype(np.float32) for t in (outer.reshape(512, 256), np.cos(twist), np.sin(twist), inner)
    )


def inverse_tables():
    inner = 2 * np.pi * (np.arange(64)[:, None] * np.arange(128) % 128) / 128
    cos, sin = np.cos(inner) / 64, np.sin(inner) / 64
    inner = np.concatenate([np.concatenate([cos, sin], 1), np.concatenate([-sin, cos], 1)], 0)
    inner = np.concatenate(split_high(inner), 0)
    k = np.broadcast_to(2 * np.arange(16)[:, None, None] + np.arange(2), (16, 4, 2)).reshape(16, 8)
    twist = 2 * np.pi * (k[:, :, None] * np.arange(128)) / 4096
    outer = np.zeros((32, 4, 2, 16, 4, 2))
    u = np.arange(32)
    for c in range(16):
        for e in range(2):
            angle = 2 * np.pi * (u * (2 * c + e) % 32) / 32
            for j in range(4):
                outer[:, j, 0, c, j, e] = np.cos(angle)
                outer[:, j, 1, c, j, e] = -np.sin(angle)
    high, low = split_high(outer.reshape(128, 256))
    outer = np.concatenate([high, high, low], 1)
    weight = np.ones((32, 128))
    weight[::2, 0] = 0.5
    return (
        inner,
        np.cos(twist).astype(np.float32),
        np.sin(twist).astype(np.float32),
        outer,
        weight.astype(ml_dtypes.bfloat16),
    )


def whiten(x_ref, outer_ref, cos_ref, sin_ref, inner_ref, white_ref):
    x = x_ref[...].reshape(16, 8, 8, 128)
    total = jnp.sum(x, axis=1)
    total = total + pltpu.roll(total, 4, 1)
    total = total + pltpu.roll(total, 2, 1)
    mean = jnp.sum(total, axis=-1, keepdims=True) * (1.0 / 4096)
    x = (x - mean[:, None]).reshape(4, 256, 128)
    row = lax.broadcasted_iota(jnp.int32, (2, 8, 128), 1)
    lane = lax.broadcasted_iota(jnp.int32, (2, 8, 128), 2)
    for half in range(2):
        both = jnp.concatenate([x[2 * half], x[2 * half + 1]], axis=1)
        section = jnp.dot(outer_ref[...], both, precision=HIGHEST, preferred_element_type=F32)
        cos, sin = cos_ref[...], sin_ref[...]
        for b in range(2):
            real = section[:256, 128 * b : 128 * b + 128]
            imag = section[256:, 128 * b : 128 * b + 128]
            turned = jnp.concatenate([real * cos + imag * sin, imag * cos - real * sin], axis=1)
            spec = jnp.dot(turned, inner_ref[...], precision=HIGHEST, preferred_element_type=F32)
            spec = spec.reshape(16, 2, 8, 128)
            power = jnp.sum(spec * spec, axis=0)
            power = power + jnp.where(row % 2 == 0, pltpu.roll(power, 7, 1), pltpu.roll(power, 1, 1))
            power = power + jnp.where(lane % 2 == 0, pltpu.roll(power, 127, 2), pltpu.roll(power, 1, 2))
            power = power + pltpu.roll(power, 64, 2)
            white = spec * (1.0 / jnp.sqrt(power * (1.0 / 64) + EPSILON))
            white_ref[:, :, 2 * half + b] = white.reshape(4, 4, 16, 128).astype(BF16)


def blocks_named(partner):
    row = lax.broadcasted_iota(jnp.int32, (SLOTS, SLOTS), 0)
    column = lax.broadcasted_iota(jnp.int32, (SLOTS, SLOTS), 1)
    partner = jnp.sum(jnp.where(row == column, partner, 0), axis=1, keepdims=True)
    source = lax.broadcasted_iota(jnp.int32, (SLOTS, 128), 1)
    named = jnp.sum(jnp.where(partner // 4 == source, partner % 4, 0), axis=0, keepdims=True)
    return jnp.broadcast_to(named, (8, 128))


def exchange_kernel(
    rows_ref, outer_ref, cos_ref, sin_ref, inner_ref, partners_ref, pairs_ref, stacked_ref, *scratch
):
    chosen, rings = scratch[:CHUNKS], scratch[CHUNKS : CHUNKS + RINGS + 1]
    near, far = rings[:2]
    load, scratch = scratch[CHUNKS + RINGS + 1 : CHUNKS + RINGS + 6], scratch[CHUNKS + RINGS + 6 :]
    white_ref, need_ref, group, picked, bounce, sides, cross, table, lookup = scratch[:9]
    load_sem, need_sem, table_sem, own_sem, y_sem, z_sem, x_sem, g_sem, c_sem, keep_sem = scratch[9:]
    sta, q = lax.axis_index("sta"), lax.axis_index("seg")
    x, z, core = sta // 16, sta // 2 % 8, sta % 2

    def at(dx, dz, flip):
        other = core if flip == 0 else 1 - core
        return (((x + dx) % NX * NZ + (z + dz) % NZ) * 2 + other, q)

    def along(dy):
        return (sta, (q + dy) % NY)

    row_peers = [(d, f) for d in range(NX) for f in range(2) if (d, f) != (0, 0)]
    up, down, right, left = at(0, 1, 0), at(0, NZ - 1, 0), at(1, 0, 0), at(NX - 1, 0, 0)
    targets = [along(r) for r in range(1, NY)] + [up, down] + [at(d, 0, f) for d, f in row_peers]
    barrier = pltpu.get_barrier_semaphore()
    for target in targets:
        pl.semaphore_signal(barrier, inc=1, device_id=target, device_id_type=MESH)
    loads = [
        pltpu.make_async_copy(source, target, load_sem.at[i])
        for i, (source, target) in enumerate(zip((rows_ref, outer_ref, cos_ref, sin_ref, inner_ref), load))
    ]
    for copy in loads:
        copy.start()
    need_ref[...] = blocks_named(partners_ref[1:2])
    table[0] = need_ref[...]
    for copy in loads:
        copy.wait()
    whiten(*load, white_ref)
    pl.semaphore_wait(barrier, len(targets))

    started = []

    def send(source, destination, sems, target):
        copy = pltpu.make_async_remote_copy(
            source, destination, sems.at[0], sems.at[1], device_id=target, device_id_type=MESH
        )
        copy.start()
        started.append(copy)
        return copy

    def sent():
        for copy in started:
            copy.wait_send()
        started.clear()

    def ring(c, dz):
        place = PLACES.index(dz)
        if c:
            return rings[c + 1].at[place]
        return near.at[place] if place < NEAR else far.at[place - NEAR]

    def home(c):
        return ring(c, 0) if c < RINGS else group.at[0, 0]

    own, y_in = {}, {}
    for c in ORDER:
        y_in[c] = [
            send(white_ref.at[(q + r) % NY, c], home(c).at[r], y_sem.at[c, r], along(r)) for r in range(1, NY)
        ]
        own[c] = pltpu.make_async_copy(white_ref.at[q, c], home(c).at[0], own_sem.at[c])
        own[c].start()
    need_in = [
        send(need_ref, table.at[d * 2 + f], need_sem.at[d * 2 + f], at(d, 0, f)) for d, f in row_peers
    ]

    def home_ready(c):
        own[c].wait()
        for copy in y_in[c]:
            copy.wait_recv()

    def landed(copies):
        for copy in copies:
            copy.wait_recv()

    hops = {}

    def hop(c, t):
        if t == 1:
            home_ready(c)
        else:
            landed(hops[c, t - 1])
        hops[c, t] = []
        if t < 4 or c % 2 == 0:
            hops[c, t].append(send(ring(c, t - 1), ring(c, t), z_sem.at[c, t], up))
        if t < 4 or c % 2 == 1:
            hops[c, t].append(send(ring(c, (9 - t) % 8), ring(c, 8 - t), z_sem.at[c, 8 - t], down))

    def pick(c, part):
        def one(slot, carry):
            for place in range(*part):
                dz = PLACES[place]
                block = lookup[slot, 0, (x * NZ + (z - dz) % NZ) * 2 + core]
                picked[c, slot, place] = ring(c, dz)[:, block]
            return carry

        if part[1] == NZ:
            landed(hops[c, 4])
        lax.fori_loop(0, 2 * NX, one, 0)
        chosen[c][0, part[0] : part[1]] = picked[c, 0, part[0] : part[1]]

    arrivals, relays = {c: [] for c in range(CHUNKS)}, {}

    def spread(c, part):
        some = slice(*part)
        sems = x_sem.at[c, int(part[0] > 0)]

        def pass_on(slot, target, sem, device):
            return send(picked.at[c, slot, some], target.at[some], sems.at[sem], device)

        relays[c, part] = [
            pass_on(4, bounce.at[c, 0], 0, right),
            pass_on(5, bounce.at[c, 1], 1, left),
        ]
        arrivals[c] += [
            pass_on(6, chosen[c].at[2], 2, right),
            pass_on(2, chosen[c].at[6], 3, left),
            pass_on(7, chosen[c].at[3], 4, at(1, 0, 1)),
            pass_on(3, chosen[c].at[7], 5, at(NX - 1, 0, 1)),
            pass_on(1, chosen[c].at[1], 6, at(0, 0, 1)),
        ]

    def forward(c, part):
        some = slice(*part)
        sems = x_sem.at[c, int(part[0] > 0)]
        relays[c, part][0].wait_recv()
        arrivals[c].append(send(bounce.at[c, 0, some], chosen[c].at[4, some], sems.at[7], right))
        relays[c, part][1].wait_recv()
        arrivals[c].append(send(bounce.at[c, 1, some], chosen[c].at[5, some], sems.at[8], at(NX - 1, 0, 1)))

    last = CHUNKS - 1
    steps = {}

    def group_start():
        home_ready(last)
        steps["x"] = [
            send(group.at[0, 0], group.at[0, 1], g_sem.at[0], right),
            send(group.at[0, 0], group.at[0, 3], g_sem.at[1], left),
        ]

    def group_across():
        steps["x"][0].wait_recv()
        one = send(group.at[0, 1, 0:2], group.at[0, 2, 0:2], g_sem.at[2], right)
        steps["x"][1].wait_recv()
        steps[0] = [one, send(group.at[0, 3, 2:4], group.at[0, 2, 2:4], g_sem.at[3], left)]

    def group_hop(t):
        landed(steps[t - 1])
        if t < 4:
            parts = (slice(0, 4), slice(0, 4))
        else:
            parts = (slice(0, 2), slice(2, 4))
        steps[t] = [
            send(group.at[t - 1, parts[0]], group.at[t, parts[0]], g_sem.at[2 * t + 2], up),
            send(group.at[(9 - t) % 8, parts[1]], group.at[8 - t, parts[1]], g_sem.at[2 * t + 3], down),
        ]

    def group_pick():
        def one(dx, carry):
            for place, dz in enumerate(PLACES):
                source = ((x - dx) % NX * NZ + (z - dz) % NZ) * 2 + core
                picked[last, dx, place] = group[dz, dx, :, lookup[1, 0, source]]
                chosen[last][dx * 2, place] = group[dz, dx, :, lookup[0, 0, source]]
            return carry

        landed(steps[4])
        lax.fori_loop(0, NX, one, 0)
        arrivals[last] += [
            send(picked.at[last, d], chosen[last].at[2 * d + 1], g_sem.at[12 + d], at(0, 0, 1)) for d in range(NX)
        ]

    row = lax.broadcasted_iota(jnp.int32, (8, 128), 0)
    first_half = lax.broadcasted_iota(jnp.int32, (8, 128), 1) < 64

    def prepare(c):
        def one(step, carry):
            b, r = step // NY, step % NY
            both = home(c)[r, b].astype(F32)
            for g in range(2):
                value = both[8 * g : 8 * g + 8]
                turned = pltpu.roll(value, 64, 1)
                for part, side in enumerate(
                    (jnp.where(first_half, value, -turned), jnp.where(first_half, turned, value))
                ):
                    for i in range(4):
                        only = jnp.where(row // 2 == i, side, 0.0)
                        only = only + pltpu.roll(only, 2, 0)
                        sides[side_of(c), b, part, i, r * 2 + g] = only + pltpu.roll(only, 4, 0)
            return carry

        lax.fori_loop(0, 4 * NY, one, 0)

    kept, handed = [], []

    def side_of(c):
        return c

    def multiply(c):
        landed(arrivals[c])
        for r in (2, 1, 3, 0):
            base = (q + r) % NY * 8

            def one(n, carry):
                slot = base + n
                first = pairs_ref[0, slot] % 4
                partner = pairs_ref[1, slot] // 4
                dx, dz, flip = (x - partner // 16) % NX, (z - partner // 2 % 8) % NZ, (core + partner) % 2
                place = jnp.where(dz == 0, 0, jnp.where(dz <= 4, 2 * dz - 1, 2 * (NZ - dz)))
                second = chosen[c][dx * 2 + flip, place].astype(F32)
                rows = []
                for i in range(4):
                    straight = sides[side_of(c), first, 0, i, 0] * second[0, 0:8]
                    crossed = sides[side_of(c), first, 1, i, 0] * second[0, 0:8]
                    for g in range(1, 8):
                        part = second[g // 2, 8 * (g % 2) : 8 * (g % 2) + 8]
                        straight = straight + sides[side_of(c), first, 0, i, g] * part
                        crossed = crossed + sides[side_of(c), first, 1, i, g] * part
                    rows.append(straight + pltpu.roll(crossed, 64, 1))
                cross[c, slot] = jnp.concatenate(rows, axis=0).astype(BF16)
                return carry

            lax.fori_loop(0, 8, one, 0, unroll=UNROLL)
            part = cross.at[c, pl.ds(base, 8)]
            if r:
                handed.append(send(part, stacked_ref.at[q, c], c_sem.at[c, r], along(r)))
            else:
                copy = pltpu.make_async_copy(part, stacked_ref.at[q, c], keep_sem.at[c])
                copy.start()
                kept.append(copy)

    near_part, far_part, whole = (0, NEAR), (NEAR, NZ), (0, NZ)
    hop(0, 1)
    group_start()
    hop(1, 1)
    prepare(0)
    hop(0, 2)
    landed(need_in)
    copy = pltpu.make_async_copy(table, lookup, table_sem)
    copy.start()
    copy.wait()
    group_across()
    hop(2, 1)
    hop(1, 2)
    hop(0, 3)
    prepare(last)
    pick(0, near_part)
    spread(0, near_part)
    hop(2, 2)
    hop(1, 3)
    prepare(1)
    hop(0, 4)
    group_hop(1)
    pick(0, far_part)
    forward(0, near_part)
    spread(0, far_part)
    hop(2, 3)
    hop(1, 4)
    prepare(2)
    pick(1, whole)
    forward(0, far_part)
    spread(1, whole)
    hop(2, 4)
    group_hop(2)
    pick(2, whole)
    group_hop(3)
    multiply(0)
    forward(1, whole)
    spread(2, whole)
    group_hop(4)
    multiply(1)
    forward(2, whole)
    group_pick()
    multiply(last)
    sent()
    multiply(2)
    for copy in kept:
        copy.wait()
    landed(handed)
    sent()


def invert_kernel(counts_ref, stacked_ref, inner_ref, cos_ref, sin_ref, outer_ref, weight_ref, out_ref):
    for n in range(STEP):
        slot = lax.axis_index("seg") * 8 + pl.program_id(0) * STEP + n
        live = (slot < counts_ref[0]).astype(F32)
        cross = stacked_ref[:, :, n].reshape(16, 32, 128)
        cross = jnp.concatenate([cross[0:1] * weight_ref[...], cross[1:]], axis=0).reshape(512, 128)
        series = jnp.dot(jnp.concatenate([cross, cross], axis=1), inner_ref[...], preferred_element_type=F32)
        series = series.reshape(16, 4, 8, 256)
        cos, sin = cos_ref[...] * live, sin_ref[...] * live
        parts = []
        for i in range(4):
            real, imag = series[:, i, :, :128], series[:, i, :, 128:]
            turned = jnp.concatenate(
                [(real * cos - imag * sin).reshape(128, 128), (real * sin + imag * cos).reshape(128, 128)], axis=0
            )
            parts.append(turned)
        for pair in range(2):
            both = jnp.concatenate([parts[2 * pair], parts[2 * pair + 1]], axis=1)
            high = both.astype(BF16)
            low = (both - high.astype(F32)).astype(BF16)
            lags = jnp.dot(
                outer_ref[...], jnp.concatenate([high, low, high], axis=0), preferred_element_type=F32
            ).astype(BF16)
            out_ref[n, 2 * pair] = lags[:, :128]
            out_ref[n, 2 * pair + 1] = lags[:, 128:]


def vmem():
    return pl.BlockSpec(memory_space=pltpu.VMEM)


def local(traces, pair_blocks, pair_counts):
    stations, segs, length = traces.shape
    rows = traces.reshape(stations, segs, 32, 128).transpose(0, 2, 1, 3).reshape(1024, 128)
    dma = pltpu.SemaphoreType.DMA
    smem = pl.BlockSpec(memory_space=pltpu.SMEM)
    stacked = pl.pallas_call(
        exchange_kernel,
        out_shape=jax.ShapeDtypeStruct((NY, CHUNKS, 8, 32, 128), BF16),
        in_specs=[pl.BlockSpec(memory_space=pltpu.HBM)] * 5 + [vmem(), smem],
        out_specs=pl.BlockSpec(memory_space=pl.ANY),
        scratch_shapes=[
            *[pltpu.VMEM((2 * NX, NZ, NY, 16, 128), BF16)] * CHUNKS,
            pltpu.VMEM((NEAR, NY, 4, 16, 128), BF16),
            pltpu.VMEM((NZ - NEAR, NY, 4, 16, 128), BF16),
            *[pltpu.VMEM((NZ, NY, 4, 16, 128), BF16)] * (RINGS - 1),
            pltpu.VMEM((1024, 128), F32),
            pltpu.VMEM((512, 256), F32),
            pltpu.VMEM((256, 128), F32),
            pltpu.VMEM((256, 128), F32),
            pltpu.VMEM((256, 128), F32),
            pltpu.VMEM((NY, CHUNKS, 4, 16, 128), BF16),
            pltpu.VMEM((8, 128), jnp.int32),
            pltpu.VMEM((NZ, NX, NY, 4, 16, 128), BF16),
            pltpu.VMEM((CHUNKS, 2 * NX, NZ, NY, 16, 128), BF16),
            pltpu.VMEM((RINGS, 2, NZ, NY, 16, 128), BF16),
            pltpu.VMEM((CHUNKS, 4, 2, 4, 8, 8, 128), F32),
            pltpu.VMEM((CHUNKS, SLOTS, 32, 128), BF16),
            pltpu.VMEM((2 * NX, 8, 128), jnp.int32),
            pltpu.SMEM((2 * NX, 8, 128), jnp.int32),
            dma((5,)),
            dma((2 * NX, 2)),
            dma(()),
            dma((CHUNKS,)),
            dma((CHUNKS, NY, 2)),
            dma((RINGS, NZ, 2)),
            dma((RINGS, 2, 9, 2)),
            dma((16, 2)),
            dma((CHUNKS, NY, 2)),
            dma((CHUNKS,)),
        ],
        compiler_params=pltpu.CompilerParams(
            collective_id=0, has_side_effects=True, vmem_limit_bytes=60 * MIB
        ),
        name="exchange",
    )(rows, *forward_tables(), pair_blocks.T, pair_blocks.T)
    whole = lambda *shape: pl.BlockSpec(shape, lambda p: (0,) * len(shape))
    lags = pl.pallas_call(
        invert_kernel,
        out_shape=jax.ShapeDtypeStruct((8, 4, 128, 128), BF16),
        grid=(8 // STEP,),
        in_specs=[
            smem,
            pl.BlockSpec((NY, CHUNKS, STEP, 32, 128), lambda p: (0, 0, p, 0, 0)),
            whole(256, 256),
            whole(16, 8, 128),
            whole(16, 8, 128),
            whole(128, 768),
            whole(32, 128),
        ],
        out_specs=pl.BlockSpec((STEP, 4, 128, 128), lambda p: (p, 0, 0, 0)),
        compiler_params=pltpu.CompilerParams(vmem_limit_bytes=32 * MIB),
        name="invert",
    )(pair_counts, stacked, *inverse_tables())
    return lags.reshape(8, 4, 32, 4, 128).transpose(0, 1, 3, 2, 4).reshape(8, 4, 4, length)


def solution(mesh):
    in_specs = (P("sta", "seg", None), P("sta", None), P("sta"))
    out_specs = P(("sta", "seg"), None, None, None)
    return jax.shard_map(local, mesh=mesh, in_specs=in_specs, out_specs=out_specs, check_vma=False)
```

```python
import functools
import math

import jax
import jax.numpy as jnp
import ml_dtypes
import numpy as np
from jax import lax
from jax.experimental import pallas as pl
from jax.experimental.pallas import tpu as pltpu
from jax.sharding import PartitionSpec as P

MESH = pl.DeviceIdType.MESH
F32 = jnp.float32
BF16 = jnp.bfloat16
HIGHEST = lax.Precision.HIGHEST
EPSILON = 1e-06
NX, NZ, NY = 4, 8, 4
CHUNKS = 4
RINGS = 3
ORDER = (0, 3, 1, 2)
PLACES = (0, 1, 7, 2, 6, 3, 5, 4)
NEAR = 5
UNROLL = 4
SLOTS = 32
STEP = 2
MIB = 1 << 20


def split_high(table):
    high = table.astype(ml_dtypes.bfloat16)
    return high, (table - high.astype(np.float64)).astype(ml_dtypes.bfloat16)


def forward_tables():
    a = np.arange(32)
    outer = np.zeros((2, 16, 2, 4, 2, 4, 32, 2))
    for c in range(16):
        for e in range(2):
            angle = 2 * np.pi * (a * (2 * c + e) % 32) / 32
            for g in range(2):
                for j in range(4):
                    outer[0, c, g, j, e, j, :, g] = np.cos(angle)
                    outer[1, c, g, j, e, j, :, g] = -np.sin(angle)
    k = np.broadcast_to(2 * np.arange(16)[:, None, None] + np.arange(2), (16, 8, 2)).reshape(256)
    twist = 2 * np.pi * (k[:, None] * np.arange(128)) / 4096
    inner = 2 * np.pi * (np.arange(128)[:, None] * np.arange(64) % 128) / 128
    cos, sin = np.cos(inner), np.sin(inner)
    inner = np.concatenate([np.concatenate([cos, -sin], 1), np.concatenate([sin, cos], 1)], 0)
    return tuple(
        t.astype(np.float32) for t in (outer.reshape(512, 256), np.cos(twist), np.sin(twist), inner)
    )


def inverse_tables():
    inner = 2 * np.pi * (np.arange(64)[:, None] * np.arange(128) % 128) / 128
    cos, sin = np.cos(inner) / 64, np.sin(inner) / 64
    inner = np.concatenate([np.concatenate([cos, sin], 1), np.concatenate([-sin, cos], 1)], 0)
    inner = np.concatenate(split_high(inner), 0)
    k = np.broadcast_to(2 * np.arange(16)[:, None, None] + np.arange(2), (16, 4, 2)).reshape(16, 8)
    twist = 2 * np.pi * (k[:, :, None] * np.arange(128)) / 4096
    outer = np.zeros((32, 4, 2, 16, 4, 2))
    u = np.arange(32)
    for c in range(16):
        for e in range(2):
            angle = 2 * np.pi * (u * (2 * c + e) % 32) / 32
            for j in range(4):
                outer[:, j, 0, c, j, e] = np.cos(angle)
                outer[:, j, 1, c, j, e] = -np.sin(angle)
    high, low = split_high(outer.reshape(128, 256))
    outer = np.concatenate([high, high, low], 1)
    weight = np.ones((32, 128))
    weight[::2, 0] = 0.5
    return (
        inner,
        np.cos(twist).astype(np.float32),
        np.sin(twist).astype(np.float32),
        outer,
        weight.astype(ml_dtypes.bfloat16),
    )


def whiten(x_ref, outer_ref, cos_ref, sin_ref, inner_ref, white_ref):
    x = x_ref[...].reshape(16, 8, 8, 128)
    total = jnp.sum(x, axis=1)
    total = total + pltpu.roll(total, 4, 1)
    total = total + pltpu.roll(total, 2, 1)
    mean = jnp.sum(total, axis=-1, keepdims=True) * (1.0 / 4096)
    x = (x - mean[:, None]).reshape(4, 256, 128)
    row = lax.broadcasted_iota(jnp.int32, (2, 8, 128), 1)
    lane = lax.broadcasted_iota(jnp.int32, (2, 8, 128), 2)
    for half in range(2):
        both = jnp.concatenate([x[2 * half], x[2 * half + 1]], axis=1)
        section = jnp.dot(outer_ref[...], both, precision=HIGHEST, preferred_element_type=F32)
        cos, sin = cos_ref[...], sin_ref[...]
        for b in range(2):
            real = section[:256, 128 * b : 128 * b + 128]
            imag = section[256:, 128 * b : 128 * b + 128]
            turned = jnp.concatenate([real * cos + imag * sin, imag * cos - real * sin], axis=1)
            spec = jnp.dot(turned, inner_ref[...], precision=HIGHEST, preferred_element_type=F32)
            spec = spec.reshape(16, 2, 8, 128)
            power = jnp.sum(spec * spec, axis=0)
            power = power + jnp.where(row % 2 == 0, pltpu.roll(power, 7, 1), pltpu.roll(power, 1, 1))
            power = power + jnp.where(lane % 2 == 0, pltpu.roll(power, 127, 2), pltpu.roll(power, 1, 2))
            power = power + pltpu.roll(power, 64, 2)
            white = spec * (1.0 / jnp.sqrt(power * (1.0 / 64) + EPSILON))
            white_ref[:, :, 2 * half + b] = white.reshape(4, 4, 16, 128).astype(BF16)


def blocks_named(partner):
    row = lax.broadcasted_iota(jnp.int32, (SLOTS, SLOTS), 0)
    column = lax.broadcasted_iota(jnp.int32, (SLOTS, SLOTS), 1)
    partner = jnp.sum(jnp.where(row == column, partner, 0), axis=1, keepdims=True)
    source = lax.broadcasted_iota(jnp.int32, (SLOTS, 128), 1)
    named = jnp.sum(jnp.where(partner // 4 == source, partner % 4, 0), axis=0, keepdims=True)
    return jnp.broadcast_to(named, (8, 128))


def exchange_kernel(
    rows_ref, outer_ref, cos_ref, sin_ref, inner_ref, partners_ref, pairs_ref, stacked_ref, *scratch
):
    chosen, rings = scratch[:CHUNKS], scratch[CHUNKS : CHUNKS + RINGS + 1]
    near, far = rings[:2]
    load, scratch = scratch[CHUNKS + RINGS + 1 : CHUNKS + RINGS + 6], scratch[CHUNKS + RINGS + 6 :]
    white_ref, need_ref, group, picked, bounce, sides, cross, table, lookup = scratch[:9]
    load_sem, need_sem, table_sem, own_sem, y_sem, z_sem, x_sem, g_sem, c_sem, keep_sem = scratch[9:]
    sta, q = lax.axis_index("sta"), lax.axis_index("seg")
    x, z, core = sta // 16, sta // 2 % 8, sta % 2

    def at(dx, dz, flip):
        other = core if flip == 0 else 1 - core
        return (((x + dx) % NX * NZ + (z + dz) % NZ) * 2 + other, q)

    def along(dy):
        return (sta, (q + dy) % NY)

    row_peers = [(d, f) for d in range(NX) for f in range(2) if (d, f) != (0, 0)]
    up, down, right, left = at(0, 1, 0), at(0, NZ - 1, 0), at(1, 0, 0), at(NX - 1, 0, 0)
    targets = [along(r) for r in range(1, NY)] + [up, down] + [at(d, 0, f) for d, f in row_peers]
    barrier = pltpu.get_barrier_semaphore()
    for target in targets:
        pl.semaphore_signal(barrier, inc=1, device_id=target, device_id_type=MESH)
    loads = [
        pltpu.make_async_copy(source, target, load_sem.at[i])
        for i, (source, target) in enumerate(zip((rows_ref, outer_ref, cos_ref, sin_ref, inner_ref), load))
    ]
    for copy in loads:
        copy.start()
    need_ref[...] = blocks_named(partners_ref[1:2])
    table[0] = need_ref[...]
    for copy in loads:
        copy.wait()
    whiten(*load, white_ref)
    pl.semaphore_wait(barrier, len(targets))

    started = []

    def send(source, destination, sems, target):
        copy = pltpu.make_async_remote_copy(
            source, destination, sems.at[0], sems.at[1], device_id=target, device_id_type=MESH
        )
        copy.start()
        started.append(copy)
        return copy

    def sent():
        for copy in started:
            copy.wait_send()
        started.clear()

    def ring(c, dz):
        place = PLACES.index(dz)
        if c:
            return rings[c + 1].at[place]
        return near.at[place] if place < NEAR else far.at[place - NEAR]

    def home(c):
        return ring(c, 0) if c < RINGS else group.at[0, 0]

    own, y_in = {}, {}
    for c in ORDER:
        y_in[c] = [
            send(white_ref.at[(q + r) % NY, c], home(c).at[r], y_sem.at[c, r], along(r)) for r in range(1, NY)
        ]
        own[c] = pltpu.make_async_copy(white_ref.at[q, c], home(c).at[0], own_sem.at[c])
        own[c].start()
    need_in = [
        send(need_ref, table.at[d * 2 + f], need_sem.at[d * 2 + f], at(d, 0, f)) for d, f in row_peers
    ]

    def home_ready(c):
        own[c].wait()
        for copy in y_in[c]:
            copy.wait_recv()

    def landed(copies):
        for copy in copies:
            copy.wait_recv()

    hops = {}

    def hop(c, t):
        if t == 1:
            home_ready(c)
        else:
            landed(hops[c, t - 1])
        hops[c, t] = []
        if t < 4 or c % 2 == 0:
            hops[c, t].append(send(ring(c, t - 1), ring(c, t), z_sem.at[c, t], up))
        if t < 4 or c % 2 == 1:
            hops[c, t].append(send(ring(c, (9 - t) % 8), ring(c, 8 - t), z_sem.at[c, 8 - t], down))

    def pick(c, part):
        def one(slot, carry):
            for place in range(*part):
                dz = PLACES[place]
                block = lookup[slot, 0, (x * NZ + (z - dz) % NZ) * 2 + core]
                picked[c, slot, place] = ring(c, dz)[:, block]
            return carry

        if part[1] == NZ:
            landed(hops[c, 4])
        lax.fori_loop(0, 2 * NX, one, 0)
        chosen[c][0, part[0] : part[1]] = picked[c, 0, part[0] : part[1]]

    arrivals, relays = {c: [] for c in range(CHUNKS)}, {}

    def spread(c, part):
        some = slice(*part)
        sems = x_sem.at[c, int(part[0] > 0)]

        def pass_on(slot, target, sem, device):
            return send(picked.at[c, slot, some], target.at[some], sems.at[sem], device)

        relays[c, part] = [
            pass_on(4, bounce.at[c, 0], 0, right),
            pass_on(5, bounce.at[c, 1], 1, left),
        ]
        arrivals[c] += [
            pass_on(6, chosen[c].at[2], 2, right),
            pass_on(2, chosen[c].at[6], 3, left),
            pass_on(7, chosen[c].at[3], 4, at(1, 0, 1)),
            pass_on(3, chosen[c].at[7], 5, at(NX - 1, 0, 1)),
            pass_on(1, chosen[c].at[1], 6, at(0, 0, 1)),
        ]

    def forward(c, part):
        some = slice(*part)
        sems = x_sem.at[c, int(part[0] > 0)]
        relays[c, part][0].wait_recv()
        arrivals[c].append(send(bounce.at[c, 0, some], chosen[c].at[4, some], sems.at[7], right))
        relays[c, part][1].wait_recv()
        arrivals[c].append(send(bounce.at[c, 1, some], chosen[c].at[5, some], sems.at[8], at(NX - 1, 0, 1)))

    last = CHUNKS - 1
    steps = {}

    def group_start():
        home_ready(last)
        steps["x"] = [
            send(group.at[0, 0], group.at[0, 1], g_sem.at[0], right),
            send(group.at[0, 0], group.at[0, 3], g_sem.at[1], left),
        ]

    def group_across():
        steps["x"][0].wait_recv()
        one = send(group.at[0, 1, 0:2], group.at[0, 2, 0:2], g_sem.at[2], right)
        steps["x"][1].wait_recv()
        steps[0] = [one, send(group.at[0, 3, 2:4], group.at[0, 2, 2:4], g_sem.at[3], left)]

    def group_hop(t):
        landed(steps[t - 1])
        if t < 4:
            parts = (slice(0, 4), slice(0, 4))
        else:
            parts = (slice(0, 2), slice(2, 4))
        steps[t] = [
            send(group.at[t - 1, parts[0]], group.at[t, parts[0]], g_sem.at[2 * t + 2], up),
            send(group.at[(9 - t) % 8, parts[1]], group.at[8 - t, parts[1]], g_sem.at[2 * t + 3], down),
        ]

    def group_pick():
        def one(dx, carry):
            for place, dz in enumerate(PLACES):
                source = ((x - dx) % NX * NZ + (z - dz) % NZ) * 2 + core
                picked[last, dx, place] = group[dz, dx, :, lookup[1, 0, source]]
                chosen[last][dx * 2, place] = group[dz, dx, :, lookup[0, 0, source]]
            return carry

        landed(steps[4])
        lax.fori_loop(0, NX, one, 0)
        arrivals[last] += [
            send(picked.at[last, d], chosen[last].at[2 * d + 1], g_sem.at[12 + d], at(0, 0, 1)) for d in range(NX)
        ]

    row = lax.broadcasted_iota(jnp.int32, (8, 128), 0)
    first_half = lax.broadcasted_iota(jnp.int32, (8, 128), 1) < 64

    def prepare(c):
        def one(step, carry):
            b, r = step // NY, step % NY
            both = home(c)[r, b].astype(F32)
            for g in range(2):
                value = both[8 * g : 8 * g + 8]
                turned = pltpu.roll(value, 64, 1)
                for part, side in enumerate(
                    (jnp.where(first_half, value, -turned), jnp.where(first_half, turned, value))
                ):
                    for i in range(4):
                        only = jnp.where(row // 2 == i, side, 0.0)
                        only = only + pltpu.roll(only, 2, 0)
                        sides[side_of(c), b, part, i, r * 2 + g] = only + pltpu.roll(only, 4, 0)
            return carry

        lax.fori_loop(0, 4 * NY, one, 0)

    kept, handed = [], []

    def side_of(c):
        return c

    def multiply(c):
        landed(arrivals[c])
        for r in (2, 1, 3, 0):
            base = (q + r) % NY * 8

            def one(n, carry):
                slot = base + n
                first = pairs_ref[0, slot] % 4
                partner = pairs_ref[1, slot] // 4
                dx, dz, flip = (x - partner // 16) % NX, (z - partner // 2 % 8) % NZ, (core + partner) % 2
                place = jnp.where(dz == 0, 0, jnp.where(dz <= 4, 2 * dz - 1, 2 * (NZ - dz)))
                second = chosen[c][dx * 2 + flip, place].astype(F32)
                rows = []
                for i in range(4):
                    straight = sides[side_of(c), first, 0, i, 0] * second[0, 0:8]
                    crossed = sides[side_of(c), first, 1, i, 0] * second[0, 0:8]
                    for g in range(1, 8):
                        part = second[g // 2, 8 * (g % 2) : 8 * (g % 2) + 8]
                        straight = straight + sides[side_of(c), first, 0, i, g] * part
                        crossed = crossed + sides[side_of(c), first, 1, i, g] * part
                    rows.append(straight + pltpu.roll(crossed, 64, 1))
                cross[c, slot] = jnp.concatenate(rows, axis=0).astype(BF16)
                return carry

            lax.fori_loop(0, 8, one, 0, unroll=UNROLL)
            part = cross.at[c, pl.ds(base, 8)]
            if r:
                handed.append(send(part, stacked_ref.at[q, c], c_sem.at[c, r], along(r)))
            else:
                copy = pltpu.make_async_copy(part, stacked_ref.at[q, c], keep_sem.at[c])
                copy.start()
                kept.append(copy)

    near_part, far_part, whole = (0, NEAR), (NEAR, NZ), (0, NZ)
    hop(0, 1)
    group_start()
    hop(1, 1)
    prepare(0)
    hop(0, 2)
    landed(need_in)
    copy = pltpu.make_async_copy(table, lookup, table_sem)
    copy.start()
    copy.wait()
    group_across()
    hop(2, 1)
    hop(1, 2)
    hop(0, 3)
    prepare(last)
    pick(0, near_part)
    spread(0, near_part)
    hop(2, 2)
    hop(1, 3)
    prepare(1)
    hop(0, 4)
    group_hop(1)
    pick(0, far_part)
    forward(0, near_part)
    spread(0, far_part)
    hop(2, 3)
    hop(1, 4)
    prepare(2)
    pick(1, whole)
    forward(0, far_part)
    spread(1, whole)
    hop(2, 4)
    group_hop(2)
    group_hop(3)
    pick(2, whole)
    multiply(0)
    forward(1, whole)
    spread(2, whole)
    group_hop(4)
    multiply(1)
    forward(2, whole)
    group_pick()
    multiply(last)
    sent()
    multiply(2)
    for copy in kept:
        copy.wait()
    landed(handed)
    sent()


def invert_kernel(counts_ref, stacked_ref, inner_ref, cos_ref, sin_ref, outer_ref, weight_ref, out_ref):
    for n in range(STEP):
        slot = lax.axis_index("seg") * 8 + pl.program_id(0) * STEP + n
        live = (slot < counts_ref[0]).astype(F32)
        cross = stacked_ref[:, :, n].reshape(16, 32, 128)
        cross = jnp.concatenate([cross[0:1] * weight_ref[...], cross[1:]], axis=0).reshape(512, 128)
        series = jnp.dot(jnp.concatenate([cross, cross], axis=1), inner_ref[...], preferred_element_type=F32)
        series = series.reshape(16, 4, 8, 256)
        cos, sin = cos_ref[...] * live, sin_ref[...] * live
        parts = []
        for i in range(4):
            real, imag = series[:, i, :, :128], series[:, i, :, 128:]
            turned = jnp.concatenate(
                [(real * cos - imag * sin).reshape(128, 128), (real * sin + imag * cos).reshape(128, 128)], axis=0
            )
            parts.append(turned)
        for pair in range(2):
            both = jnp.concatenate([parts[2 * pair], parts[2 * pair + 1]], axis=1)
            high = both.astype(BF16)
            low = (both - high.astype(F32)).astype(BF16)
            lags = jnp.dot(
                outer_ref[...], jnp.concatenate([high, low, high], axis=0), preferred_element_type=F32
            ).astype(BF16)
            out_ref[n, 2 * pair] = lags[:, :128]
            out_ref[n, 2 * pair + 1] = lags[:, 128:]


def vmem():
    return pl.BlockSpec(memory_space=pltpu.VMEM)


def local(traces, pair_blocks, pair_counts):
    stations, segs, length = traces.shape
    rows = traces.reshape(stations, segs, 32, 128).transpose(0, 2, 1, 3).reshape(1024, 128)
    dma = pltpu.SemaphoreType.DMA
    smem = pl.BlockSpec(memory_space=pltpu.SMEM)
    stacked = pl.pallas_call(
        exchange_kernel,
        out_shape=jax.ShapeDtypeStruct((NY, CHUNKS, 8, 32, 128), BF16),
        in_specs=[pl.BlockSpec(memory_space=pltpu.HBM)] * 5 + [vmem(), smem],
        out_specs=pl.BlockSpec(memory_space=pl.ANY),
        scratch_shapes=[
            *[pltpu.VMEM((2 * NX, NZ, NY, 16, 128), BF16)] * CHUNKS,
            pltpu.VMEM((NEAR, NY, 4, 16, 128), BF16),
            pltpu.VMEM((NZ - NEAR, NY, 4, 16, 128), BF16),
            *[pltpu.VMEM((NZ, NY, 4, 16, 128), BF16)] * (RINGS - 1),
            pltpu.VMEM((1024, 128), F32),
            pltpu.VMEM((512, 256), F32),
            pltpu.VMEM((256, 128), F32),
            pltpu.VMEM((256, 128), F32),
            pltpu.VMEM((256, 128), F32),
            pltpu.VMEM((NY, CHUNKS, 4, 16, 128), BF16),
            pltpu.VMEM((8, 128), jnp.int32),
            pltpu.VMEM((NZ, NX, NY, 4, 16, 128), BF16),
            pltpu.VMEM((CHUNKS, 2 * NX, NZ, NY, 16, 128), BF16),
            pltpu.VMEM((RINGS, 2, NZ, NY, 16, 128), BF16),
            pltpu.VMEM((CHUNKS, 4, 2, 4, 8, 8, 128), F32),
            pltpu.VMEM((CHUNKS, SLOTS, 32, 128), BF16),
            pltpu.VMEM((2 * NX, 8, 128), jnp.int32),
            pltpu.SMEM((2 * NX, 8, 128), jnp.int32),
            dma((5,)),
            dma((2 * NX, 2)),
            dma(()),
            dma((CHUNKS,)),
            dma((CHUNKS, NY, 2)),
            dma((RINGS, NZ, 2)),
            dma((RINGS, 2, 9, 2)),
            dma((16, 2)),
            dma((CHUNKS, NY, 2)),
            dma((CHUNKS,)),
        ],
        compiler_params=pltpu.CompilerParams(
            collective_id=0, has_side_effects=True, vmem_limit_bytes=60 * MIB
        ),
        name="exchange",
    )(rows, *forward_tables(), pair_blocks.T, pair_blocks.T)
    whole = lambda *shape: pl.BlockSpec(shape, lambda p: (0,) * len(shape))
    lags = pl.pallas_call(
        invert_kernel,
        out_shape=jax.ShapeDtypeStruct((8, 4, 128, 128), BF16),
        grid=(8 // STEP,),
        in_specs=[
            smem,
            pl.BlockSpec((NY, CHUNKS, STEP, 32, 128), lambda p: (0, 0, p, 0, 0)),
            whole(256, 256),
            whole(16, 8, 128),
            whole(16, 8, 128),
            whole(128, 768),
            whole(32, 128),
        ],
        out_specs=pl.BlockSpec((STEP, 4, 128, 128), lambda p: (p, 0, 0, 0)),
        compiler_params=pltpu.CompilerParams(vmem_limit_bytes=32 * MIB),
        name="invert",
    )(pair_counts, stacked, *inverse_tables())
    return lags.reshape(8, 4, 32, 4, 128).transpose(0, 1, 3, 2, 4).reshape(8, 4, 4, length)


def solution(mesh):
    in_specs = (P("sta", "seg", None), P("sta", None), P("sta"))
    out_specs = P(("sta", "seg"), None, None, None)
    return jax.shard_map(local, mesh=mesh, in_specs=in_specs, out_specs=out_specs, check_vma=False)
```
